512 devices in a mesh: tm: 64 (over x, z, core), panel: 8 (over y).
Axes of the slice: x: 4, y: 8, z: 8, core: 2. Of those that a mesh axis runs over, the one named last changes fastest.
Arguments:
- transition: bfloat16 [64, 1024, 1024], P('tm', None, 'panel'), may hold values from -1 to 1
- drift: bfloat16 [64, 1024], P('tm'), may hold values from -6 to 6
- spread: bfloat16 [64, 1024, 1024], P('tm', None, 'panel'), may hold values from -1 to 1, as said below
- belief: bfloat16 [64, 1024], P('tm'), may hold values from -6 to 6
- precision: bfloat16 [64, 1024, 1024], P('tm', None, 'panel'), may hold values from -1 to 1, as said below
- probe_hosts: int32 [64, 256], P('tm'), may hold values from 0 to 511
- probe_values: float32 [64, 256], P('tm'), may hold values from -6 to 6
Outputs:
- sum_transition: bfloat16 [64, 1024, 1024], P('tm', None, 'panel')
- sum_drift: bfloat16 [64, 1024], P('tm')
- sum_spread: bfloat16 [64, 1024, 1024], P('tm', None, 'panel')
- sum_belief: bfloat16 [64, 1024], P('tm')
- sum_precision: bfloat16 [64, 1024, 1024], P('tm', None, 'panel')
The draws below stay inside these ranges and needn't reach their ends.
Inputs may be any that keep to these rules, and one draw needn't show every extreme that they name: `spread`: every 1024 x 1024 block is symmetric. `precision`: every 1024 x 1024 block is symmetric.
All inputs are finite; a program needn't handle non-finite values.
Results may differ from the reference program's by a relative error of at most 0.012.
The reference program's roundings to bfloat16 on the way count: a program that leaves them out, or rounds other values in their place, can miss the bound.
Values may be sent and summed in bfloat16 or wider, within the bound.
No kernel may reach another device: no remote copies, remote signals or barrier semaphores. Data moves between devices by JAX's collectives and lax.ppermute only.
A program may use at most 64 MiB of HBM per device.

```python
import math
import jax
import jax.numpy as jnp
from jax import lax

D = 1024
HOSTS = 512
NS = 2
LEVELS = 2
PROBES = 256
N_TM = 64


def dense_noise(key, symmetric):
    noise = jnp.clip(jax.random.normal(key, (N_TM, D, D), jnp.float32), -5.0, 5.0)
    if symmetric:
        noise = (noise + jnp.swapaxes(noise, 1, 2)) * math.sqrt(0.5)
    return noise


def identity_mask():
    row_ids = lax.broadcasted_iota(jnp.int32, (D, D), 0)
    col_ids = lax.broadcasted_iota(jnp.int32, (D, D), 1)
    return (row_ids == col_ids).astype(jnp.float32)


def diagonal_block(key, lowest, highest, noise_scale):
    first_key, second_key = jax.random.split(key)
    diag_values = jax.random.uniform(first_key, (N_TM, D, 1), jnp.float32, lowest, highest)
    noise = dense_noise(second_key, True)
    matrix = diag_values * identity_mask() + noise * (noise_scale / math.sqrt(D))
    return jnp.clip(matrix, -0.99, 0.99)


def draw_transition(key, part):
    base = jax.random.fold_in(key, 101)
    keep_key, skew_key, step_key, noise_key = jax.random.split(base, 4)
    offset_keep = jax.random.uniform(keep_key, (N_TM, D, 1), jnp.float32, 0.5, 0.85)
    skew_keep = jax.random.uniform(skew_key, (N_TM, D, 1), jnp.float32, 0.7, 0.95)
    step_length = jax.random.uniform(step_key, (N_TM, D, 1), jnp.float32, 0.3, 0.7)
    row_ids = lax.broadcasted_iota(jnp.int32, (D, D), 0)
    col_ids = lax.broadcasted_iota(jnp.int32, (D, D), 1)
    even_rows = lax.broadcasted_iota(jnp.int32, (D, 1), 0) % 2 == 0
    upper_mask = ((row_ids % 2 == 0) & (col_ids == row_ids + 1)).astype(jnp.float32)
    keep_values = jnp.where(even_rows, offset_keep, skew_keep)
    noise = dense_noise(noise_key, False)
    matrix = keep_values * identity_mask() + offset_keep * step_length * upper_mask + noise * (0.25 / math.sqrt(D))
    return jnp.clip(matrix, -0.99, 0.99).astype(jnp.bfloat16)


def draw_spread(key, part):
    return diagonal_block(jax.random.fold_in(key, 202), 0.5, 0.85, 0.15).astype(jnp.bfloat16)


def draw_precision(key, part):
    return diagonal_block(jax.random.fold_in(key, 303), 0.45, 0.8, 0.13).astype(jnp.bfloat16)


def plant(result, own_key, low, high):
    spot = [jax.random.randint(jax.random.fold_in(own_key, axis), (), 0, length) for axis, length in enumerate(result.shape)]
    longest = result.shape.index(max(result.shape))
    beside = spot[:longest] + [(spot[longest] + 1) % result.shape[longest]] + spot[longest + 1:]
    return result.at[tuple(spot)].set(low).at[tuple(beside)].set(high)


def levels(stream_key, dims, cuts, least, largest):
    loudness, own = 1.0, jax.random.fold_in(stream_key, 6)
    for position, parts in cuts:
        draws = jnp.exp(jax.random.uniform(jax.random.fold_in(own, position), (parts,), jnp.float32, least / len(cuts), largest / len(cuts)))
        loudness = loudness * jnp.repeat(draws, dims[position] // parts).reshape([-1 if axis == position else 1 for axis in range(len(dims))])
    return loudness


def bell_draw(own_key, shape, scale, most, cuts=(), held_as=jnp.bfloat16):
    entries = scale * jax.random.normal(own_key, shape, jnp.float32)
    if cuts:
        entries = entries * levels(own_key, shape, cuts, -0.22, 0.18)
    return jnp.clip(entries, -most, most).astype(held_as)


def setup_inputs(seed: int = 0) -> dict:
    arg_keys = jax.random.split(jax.random.key(seed), 8)
    transition = draw_transition(jax.random.fold_in(arg_keys[7], 71), 0)
    drift = bell_draw(arg_keys[1], (N_TM, D), 1.0, 6.0, ((0, 64),))
    spread = draw_spread(jax.random.fold_in(arg_keys[7], 71), 0)
    belief = bell_draw(arg_keys[3], (N_TM, D), 1.0, 6.0, ((0, 64),))
    precision = draw_precision(jax.random.fold_in(arg_keys[7], 71), 0)
    probe_hosts = plant(jax.random.randint(arg_keys[5], (N_TM, PROBES), 0, HOSTS), jax.random.fold_in(arg_keys[5], 1), 0, HOSTS - 1).astype(jnp.int32)
    probe_values = bell_draw(arg_keys[6], (N_TM, PROBES), 1.0, 6.0, ((0, 64),), jnp.float32)
    return dict(transition=transition, drift=drift, spread=spread, belief=belief, precision=precision, probe_hosts=probe_hosts, probe_values=probe_values)


def mat_vector(matrix, vector):
    return jnp.dot(matrix, vector.astype(jnp.bfloat16), preferred_element_type=jnp.float32)


def tmat_vector(matrix, vector):
    return jnp.dot(vector.astype(jnp.bfloat16), matrix, preferred_element_type=jnp.float32)


def series_panel(cov_full, info_full, anchor, series_terms):
    current = anchor
    for repeat in range(series_terms):
        inside = jnp.dot(info_full, current, preferred_element_type=jnp.float32).astype(jnp.bfloat16)
        outside = jnp.dot(cov_full, inside, preferred_element_type=jnp.float32)
        current = (anchor.astype(jnp.float32) - outside).astype(jnp.bfloat16)
    return current


def series_forward(cov_full, info_full, anchor, series_terms):
    current = anchor
    for repeat in range(series_terms):
        current = anchor - mat_vector(cov_full, mat_vector(info_full, current))
    return current


def series_backward(cov_full, info_full, anchor, series_terms):
    current = anchor
    for repeat in range(series_terms):
        current = anchor - mat_vector(info_full, mat_vector(cov_full, current))
    return current


def combine(earlier, latter):
    move_early, drift_early, spread_early, belief_early, weight_early = earlier
    move_late, drift_late, spread_late, belief_late, weight_late = latter
    series_terms = 2 ** NS - 1
    crossed = lax.dot_general(spread_early, move_late, (((1,), (1,)), ((), ())), preferred_element_type=jnp.float32).astype(jnp.bfloat16)
    carried = series_panel(spread_early, weight_late, move_early, series_terms)
    widened = series_panel(spread_early, weight_late, crossed, series_terms)
    move_new = jnp.dot(move_late, carried, preferred_element_type=jnp.float32).astype(jnp.bfloat16)
    spread_new = (jnp.dot(move_late, widened, preferred_element_type=jnp.float32) + spread_late.astype(jnp.float32)).astype(jnp.bfloat16)
    weighted = jnp.dot(weight_late, carried, preferred_element_type=jnp.float32).astype(jnp.bfloat16)
    weight_new = (lax.dot_general(move_early, weighted, (((0,), (0,)), ((), ())), preferred_element_type=jnp.float32) + weight_early.astype(jnp.float32)).astype(jnp.bfloat16)
    forward = drift_early.astype(jnp.float32) + mat_vector(spread_early, belief_late)
    forward = series_forward(spread_early, weight_late, forward, series_terms)
    drift_new = (mat_vector(move_late, forward) + drift_late.astype(jnp.float32)).astype(jnp.bfloat16)
    backward = belief_late.astype(jnp.float32) - mat_vector(weight_late, drift_early)
    backward = series_backward(spread_early, weight_late, backward, series_terms)
    belief_new = (tmat_vector(move_early, backward) + belief_early.astype(jnp.float32)).astype(jnp.bfloat16)
    return move_new, drift_new, spread_new, belief_new, weight_new


def combine_matched(matched):
    return combine(matched[0], matched[1])


def reference(transition, drift, spread, belief, precision, probe_hosts, probe_values):
    slab_rows = jnp.arange(N_TM, dtype=jnp.int32)[:, None] * jnp.ones_like(probe_hosts)
    offsets = jnp.zeros((N_TM, HOSTS), jnp.float32).at[slab_rows, probe_hosts].add(probe_values)
    paired = jnp.stack([offsets, jnp.zeros_like(offsets)], axis=2).reshape(N_TM, D)
    belief_start = (belief.astype(jnp.float32) + paired).astype(jnp.bfloat16)
    elements = (transition, drift, spread, belief_start, precision)
    for height in range(LEVELS):
        earlier = tuple(member[0::2] for member in elements)
        latter = tuple(member[1::2] for member in elements)
        elements = lax.map(combine_matched, (earlier, latter))
    copies = 2 ** LEVELS
    outcome = tuple(jnp.repeat(member, copies, axis=0) for member in elements)
    return outcome[0], outcome[1], outcome[2], outcome[3], outcome[4]
```

```python
import jax
import jax.numpy as jnp
from jax import lax
from jax.experimental import pallas as pl
from jax.experimental.pallas import tpu as pltpu
from jax.sharding import PartitionSpec as P

NS = 2
LEVELS = 2
W = 128
N = 8
D = W * N
RING = 1664
HALF = 768
INTERPRET = False

f32 = jnp.float32
bf16 = jnp.bfloat16


def dot(a, b):
    return jnp.dot(a, b, preferred_element_type=f32)


def eye_mask():
    return lax.broadcasted_iota(jnp.int32, (W, W), 0) == lax.broadcasted_iota(jnp.int32, (W, W), 1)


def as_column(row, eye):
    col = jnp.sum(jnp.where(eye, jnp.broadcast_to(row, (W, W)), 0.0), axis=1, keepdims=True)
    return jnp.broadcast_to(col, (W, W))


def as_row(block, eye):
    return jnp.sum(jnp.where(eye, block, 0.0), axis=0, keepdims=True)


def call(kernel, out_shape, scratch, scalars, *args):
    outs = out_shape if isinstance(out_shape, (list, tuple)) else [out_shape]
    vm = pl.BlockSpec(memory_space=pltpu.VMEM)
    res = pl.pallas_call(
        kernel,
        out_shape=list(outs),
        in_specs=[pl.BlockSpec(memory_space=pltpu.SMEM)] + [vm] * len(args),
        out_specs=[vm] * len(outs),
        scratch_shapes=list(scratch),
        compiler_params=pltpu.CompilerParams(vmem_limit_bytes=56 * 2**20),
        interpret=INTERPRET,
    )(scalars, *args)
    return res


def struct(*shape):
    return jax.ShapeDtypeStruct(shape, bf16)


def blk(index):
    return pl.ds(pl.multiple_of(index * W, W), W)


def start_kernel(s, spread, weight, drift, belief, hosts, values, msg, own_vec):
    role = s[0]

    @pl.when(role == 0)
    def _():
        msg[0:D, :] = weight[...]

    @pl.when(role == 1)
    def _():
        msg[0:D, :] = spread[...]

    state = lax.broadcasted_iota(jnp.int32, (hosts.shape[0], D), 1)
    hit = jnp.where(2 * hosts[...] == state, values[...], 0.0)
    eta = (belief[...].astype(f32) + jnp.sum(hit, axis=0, keepdims=True)).astype(bf16).astype(f32)
    b = drift[...].astype(f32)
    rows = [b[:, k * W : (k + 1) * W] for k in range(N)] + [
        eta[:, k * W : (k + 1) * W] for k in range(N)
    ]
    vec = jnp.concatenate(rows, axis=0).astype(bf16)
    msg[D : D + 2 * N, :] = vec
    own_vec[...] = vec


def ring_kernel(s, xa, xb, aa, ab, msg):
    q = s[1]

    def put_x(src):
        for d in range(4):
            msg[512 + d * W : 512 + (d + 1) * W, :] = src[blk((q + d) % N), :]
        msg[1536:1664, :] = src[blk((q + 4) % N), :]

    def put_a(src):
        msg[0:512, :] = src[0:512, :]
        msg[1024:1536, :] = src[512:1024, :]

    pl.when(s[2] == 0)(lambda: put_x(xa))
    pl.when(s[2] == 1)(lambda: put_x(xb))
    pl.when(s[3] == 0)(lambda: put_a(aa))
    pl.when(s[3] == 1)(lambda: put_a(ab))


def assemble_kernel(s, xa, xb, msg, m1, m2, m3, p1, p2, p3, m4, p4, x_out, a_out):
    q = s[1]

    def put(l, d, block):
        r = (l + d) % N
        x_out[r * W : (r + 1) * W, l * W : (l + 1) * W] = block
        if d:
            x_out[l * W : (l + 1) * W, r * W : (r + 1) * W] = block.T

    def own(src):
        for d in range(N):
            put(0, d, src[blk((q + d) % N), :])

    pl.when(s[2] == 0)(lambda: own(xa))
    pl.when(s[2] == 1)(lambda: own(xb))
    for l, src in ((1, m1), (2, m2), (3, m3), (7, p1), (6, p2), (5, p3)):
        for d in range(5 if l < 4 else 4):
            if (l + d) % N == 0:
                continue
            row = 1536 if d == 4 else 512 + d * W
            put(l, d, src[row : row + W, :])
    for d in (0, 1):
        put(4, d, m4[512 + d * W : 512 + (d + 1) * W, :])
        put(4, d + 2, p4[d * W : (d + 1) * W, :])
    for l, src in ((0, msg), (1, m1), (2, m2), (3, m3), (7, p1), (6, p2), (5, p3)):
        a_out[0:512, l * W : (l + 1) * W] = src[0:512, :]
        a_out[512:1024, l * W : (l + 1) * W] = src[1024:1536, :]
    a_out[0:512, 4 * W : 5 * W] = m4[0:512, :]
    a_out[512:1024, 4 * W : 5 * W] = p4[256:768, :]


def combine_kernel(
    s, x_own, x_other, a_full, aia, aib, adda, addb, vec_i, vec_j, out1, out2, r, t, base, acc, vecs
):
    role = s[0]
    q = s[1]
    terms = 2**NS - 1
    eye = eye_mask()
    vi = vec_i[...].astype(f32)
    vj = vec_j[...].astype(f32)

    def rotated_move(dst, col):
        def put(src):
            for l in range(N):
                dst[l * W : (l + 1) * W, col : col + W] = src[blk((q + l) % N), :]

        pl.when(s[2] == 0)(lambda: put(aia))
        pl.when(s[2] == 1)(lambda: put(aib))

    def rotated_vector(rows, first, dst, col):
        vecs[...] = rows
        for l in range(N):
            row = vecs[pl.ds(first + (q + l) % N, 1), :]
            dst[l * W : (l + 1) * W, col : col + W] = as_column(row, eye).astype(dst.dtype)

    @pl.when(role == 0)
    def _():
        cov, info = x_own, x_other
        a_row = a_full[blk(q), :]
        for l in range(N):
            r[l * W : (l + 1) * W, 0:W] = a_row[:, l * W : (l + 1) * W].T
        rotated_vector(vj, N, r, 2 * W)
        rotated_vector(vi, 0, acc, 0)
        v = dot(cov[...], r[:, 0:W]).astype(bf16)
        w = acc[:, 0:W] + dot(cov[...], r[:, 2 * W : 3 * W])
        acc[:, 0:W] = w
        base[:, 0:W] = v
        rotated_move(base, W)
        r[:, 0 : 2 * W] = base[...]
        r[:, 2 * W : 3 * W] = w.astype(bf16)
        for _ in range(terms):
            t[...] = dot(info[...], r[...]).astype(bf16)
            out = dot(cov[...], t[...])
            r[:, 0 : 2 * W] = (base[...].astype(f32) - out[:, 0 : 2 * W]).astype(bf16)
            r[:, 2 * W : 3 * W] = (acc[:, 0:W] - out[:, 2 * W : 3 * W]).astype(bf16)
        res = dot(a_full[...], r[...])

        def put_c(src):
            out1[0:D, :] = (res[:, 0:W] + src[0:D, :].astype(f32)).astype(bf16)

        pl.when(s[3] == 0)(lambda: put_c(adda))
        pl.when(s[3] == 1)(lambda: put_c(addb))
        out2[...] = res[:, W : 2 * W].astype(bf16)
        rows = [
            as_row(res[l * W : (l + 1) * W, 2 * W : 3 * W], eye) + vj[l : l + 1, :] for l in range(N)
        ]
        rows = rows + [jnp.zeros((1, W), f32)] * N
        out1[D : D + 2 * N, :] = jnp.concatenate(rows, axis=0).astype(bf16)

    @pl.when(role == 1)
    def _():
        info, cov = x_own, x_other
        rotated_move(base, 0)
        rotated_vector(vi, 0, r, W)
        rotated_vector(vj, N, acc, 0)
        r[:, 0:W] = base[:, 0:W]
        out = dot(info[...], r[:, 0 : 2 * W])
        back = acc[:, 0:W] - out[:, W : 2 * W]
        acc[:, 0:W] = back
        t[:, 0:W] = out[:, 0:W].astype(bf16)
        t[:, W : 2 * W] = back.astype(bf16)
        for _ in range(terms):
            out = dot(cov[...], t[:, 0 : 2 * W])
            r[:, 0:W] = (base[:, 0:W].astype(f32) - out[:, 0:W]).astype(bf16)
            r[:, W : 2 * W] = out[:, W : 2 * W].astype(bf16)
            out = dot(info[...], r[:, 0 : 2 * W])
            t[:, 0:W] = out[:, 0:W].astype(bf16)
            t[:, W : 2 * W] = (acc[:, 0:W] - out[:, W : 2 * W]).astype(bf16)
        for l in range(N):
            r[blk((q + l) % N), 0 : 2 * W] = t[l * W : (l + 1) * W, 0 : 2 * W]
        res = dot(r[:, 0 : 2 * W].T, a_full[...])
        acc[0 : 2 * W, :] = res

        def put_j(src):
            for l in range(N):
                rows = blk((q + l) % N)
                out1[rows, :] = (
                    acc[0:W, l * W : (l + 1) * W].T + src[rows, :].astype(f32)
                ).astype(bf16)

        pl.when(s[3] == 0)(lambda: put_j(adda))
        pl.when(s[3] == 1)(lambda: put_j(addb))
        vecs[...] = vi
        for l in range(N):
            spot = pl.ds(N + (q + l) % N, 1)
            vecs[spot, :] = vecs[spot, :] + acc[W : W + 1, l * W : (l + 1) * W]
        rows = lax.broadcasted_iota(jnp.int32, (2 * N, W), 0)
        out1[D : D + 2 * N, :] = jnp.where(rows < N, 0.0, vecs[...]).astype(bf16)
        out2[...] = jnp.zeros((D, W), bf16)


def finish_kernel(s, own1, own2, got1, got2, move, spread, weight, drift, belief):
    def put(first, second_move, last):
        spread[...] = first[0:D, :]
        move[...] = second_move[...]
        weight[...] = last[0:D, :]
        b = first[D : D + 2 * N, :].astype(f32)
        e = last[D : D + 2 * N, :].astype(f32)
        for l in range(N):
            drift[:, l * W : (l + 1) * W] = b[l : l + 1, :].astype(bf16)
            belief[:, l * W : (l + 1) * W] = e[N + l : N + l + 1, :].astype(bf16)

    pl.when(s[0] == 0)(lambda: put(own1, own2, got1))
    pl.when(s[0] == 1)(lambda: put(got1, got2, own1))


def swap(x, axis_bit):
    return lax.ppermute(x, "tm", [(i, i ^ (1 << axis_bit)) for i in range(lax.axis_size("tm"))])


def swap_early(x, axis_bit):
    return lax.ppermute(x, "tm", [(i, i ^ (1 << axis_bit)) for i in range(0, lax.axis_size("tm"), 2)])


def send_early(x):
    return lax.ppermute(x, "tm", [(i, i + 1) for i in range(0, lax.axis_size("tm"), 2)])


def shift(x, by):
    return lax.ppermute(x, "panel", [(i, (i + by) % N) for i in range(N)])


def gathered(msg):
    up, down = msg, msg
    got_m, got_p = [], []
    for _ in range(3):
        up = shift(up, 1)
        down = shift(down, -1)
        got_p.append(up)
        got_m.append(down)
    m4 = shift(down[0:HALF], -1)
    p4 = shift(up[HALF : 2 * HALF], 1)
    return got_m + got_p + [m4, p4]


def combined(role, q, x_pair, x_pick, ring_pair, ring_pick, ai_pair, ai_pick, add_pair, add_pick, vec_i, vec_j):
    ring_scalars = jnp.stack([role, q, x_pick, ring_pick])
    (msg,) = call(ring_kernel, [struct(RING, W)], (), ring_scalars, *x_pair, *ring_pair)
    parts = gathered(msg)
    x_full, a_full = call(
        assemble_kernel, [struct(D, D), struct(D, D)], (), ring_scalars, *x_pair, msg, *parts
    )
    x_other = swap(x_full, 0)
    return call(
        combine_kernel,
        [struct(D + 2 * N, W), struct(D, W)],
        (
            pltpu.VMEM((D, 3 * W), bf16),
            pltpu.VMEM((D, 3 * W), bf16),
            pltpu.VMEM((D, 2 * W), bf16),
            pltpu.VMEM((D, D), f32),
            pltpu.VMEM((2 * N, W), f32),
        ),
        jnp.stack([role, q, ai_pick, add_pick]),
        x_full,
        x_other,
        a_full,
        *ai_pair,
        *add_pair,
        vec_i,
        vec_j,
    )


def local(transition, drift, spread, belief, precision, probe_hosts, probe_values):
    q = lax.axis_index("panel").astype(jnp.int32)
    t = lax.axis_index("tm").astype(jnp.int32)
    role = t & 1
    odd = (t >> 1) & 1
    zero = jnp.zeros((), jnp.int32)
    move, cov, info = transition[0], spread[0], precision[0]
    first, own_vec = call(
        start_kernel,
        [struct(D + 2 * N, W), struct(2 * N, W)],
        (),
        jnp.stack([role, q]),
        cov,
        info,
        drift,
        belief,
        probe_hosts.reshape(-1, 1),
        probe_values.reshape(-1, 1),
    )
    got_move = swap(move, 0)
    got = swap(first, 0)
    got_vec = got[D:]
    vec_i = jnp.where(role == 0, own_vec, got_vec)
    vec_j = jnp.where(role == 0, got_vec, own_vec)
    out1, out2 = combined(
        role, q, (cov, info), role, (got_move, got_move), zero, (move, got_move), role,
        (got, got), zero, vec_i, vec_j,
    )
    far1 = swap(out1, 1)
    far2 = swap_early(out2, 1)
    near = odd == 0
    pair_i = jnp.where(near, out1[D:], far1[D:])
    pair_j = jnp.where(near, far1[D:], out1[D:])
    early_move = jnp.where(near, out2, far2)
    bundle = swap(jnp.concatenate([early_move, pair_i, pair_j], axis=0), 0)
    vec_i = pair_i + bundle[D : D + 2 * N]
    vec_j = pair_j + bundle[D + 2 * N :]
    late_move = jnp.where(near, far2, out2)
    out1, out2 = combined(
        role, q, (out1, far1), role ^ odd, (late_move, bundle), role, (early_move, bundle), role,
        (far1, out1), role ^ odd, vec_i, vec_j,
    )
    got1 = swap(out1, 0)
    got2 = send_early(out2)
    panel = struct(D, W)
    row = struct(1, D)
    move, cov, info, drift, belief = call(
        finish_kernel, [panel, panel, panel, row, row], (), jnp.stack([role, q]), out1, out2, got1, got2
    )
    return move[None], drift, cov[None], belief, info[None]


def solution(mesh):
    in_specs = (
        P("tm", None, "panel"),
        P("tm", None),
        P("tm", None, "panel"),
        P("tm", None),
        P("tm", None, "panel"),
        P("tm", None),
        P("tm", None),
    )
    out_specs = (
        P("tm", None, "panel"),
        P("tm", None),
        P("tm", None, "panel"),
        P("tm", None),
        P("tm", None, "panel"),
    )
    return jax.shard_map(local, mesh=mesh, in_specs=in_specs, out_specs=out_specs, check_vma=False)
```

```python
import jax
import jax.numpy as jnp
from jax import lax
from jax.experimental import pallas as pl
from jax.experimental.pallas import tpu as pltpu
from jax.sharding import PartitionSpec as P

NS = 2
LEVELS = 2
W = 128
N = 8
D = W * N
RING = 1664
HALF = 768
INTERPRET = False

f32 = jnp.float32
bf16 = jnp.bfloat16


def dot(a, b):
    return jnp.dot(a, b, preferred_element_type=f32)


def call(kernel, out_shape, scratch, scalars, *args, vmem=None, vmem_out=True):
    vm = pl.BlockSpec(memory_space=pltpu.VMEM)
    hbm = pl.BlockSpec(memory_space=pl.ANY)
    staged = len(args) if vmem is None else vmem
    outs = list(out_shape)
    flags = vmem_out if isinstance(vmem_out, (list, tuple)) else [vmem_out] * len(outs)
    return pl.pallas_call(
        kernel,
        out_shape=outs,
        in_specs=[pl.BlockSpec(memory_space=pltpu.SMEM)]
        + [vm] * staged
        + [hbm] * (len(args) - staged),
        out_specs=[vm if flag else hbm for flag in flags],
        scratch_shapes=list(scratch),
        compiler_params=pltpu.CompilerParams(vmem_limit_bytes=56 * 2**20),
        interpret=INTERPRET,
    )(scalars, *args)


def struct(*shape):
    return jax.ShapeDtypeStruct(shape, bf16)


def blk(index):
    return pl.ds(pl.multiple_of(index * W, W), W)


def start_kernel(s, spread, weight, drift, belief, hosts, values, msg, own_vec):
    role = s[0]

    @pl.when(role == 0)
    def _():
        msg[0:D, :] = weight[...]

    @pl.when(role == 1)
    def _():
        msg[0:D, :] = spread[...]

    state = lax.broadcasted_iota(jnp.int32, (hosts.shape[0], D), 1)
    hit = jnp.where(2 * hosts[...] == state, values[...], 0.0)
    eta = (belief[...].astype(f32) + jnp.sum(hit, axis=0, keepdims=True)).astype(bf16).astype(f32)
    b = drift[...].astype(f32)
    rows = [b[:, k * W : (k + 1) * W] for k in range(N)] + [
        eta[:, k * W : (k + 1) * W] for k in range(N)
    ]
    vec = jnp.concatenate(rows, axis=0).astype(bf16)
    msg[D : D + 2 * N, :] = vec
    own_vec[...] = vec


def run_copies(copies):
    for c in copies:
        c.start()
    for c in copies:
        c.wait()


def ring_kernel(s, xa, xb, aa, ab, msg, sems):
    q = s[1]

    def x_copies(src):
        out = [
            pltpu.make_async_copy(src.at[blk((q + d) % N)], msg.at[pl.ds(512 + d * W, W)], sems.at[d])
            for d in range(4)
        ]
        return out + [
            pltpu.make_async_copy(src.at[blk((q + 4) % N)], msg.at[pl.ds(1536, W)], sems.at[4])
        ]

    def a_copies(src):
        return [
            pltpu.make_async_copy(src.at[pl.ds(0, 512)], msg.at[pl.ds(0, 512)], sems.at[5]),
            pltpu.make_async_copy(src.at[pl.ds(512, 512)], msg.at[pl.ds(1024, 512)], sems.at[6]),
        ]

    for i, x in ((0, xa), (1, xb)):
        for j, a in ((0, aa), (1, ab)):
            pl.when((s[2] == i) & (s[3] == j))(lambda x=x, a=a: run_copies(x_copies(x) + a_copies(a)))


def assemble_kernel(s, xa, xb, m1, m2, m3, p1, p2, p3, m4, p4, x_out):
    q = s[1]

    def put(l, d, block):
        r = (l + d) % N
        x_out[r * W : (r + 1) * W, l * W : (l + 1) * W] = block
        if d:
            x_out[l * W : (l + 1) * W, r * W : (r + 1) * W] = block.T

    def own(src):
        for d in range(N):
            put(0, d, src[blk((q + d) % N), :])

    pl.when(s[2] == 0)(lambda: own(xa))
    pl.when(s[2] == 1)(lambda: own(xb))
    for l, src in ((1, m1), (2, m2), (3, m3), (7, p1), (6, p2), (5, p3)):
        for d in range(5 if l < 4 else 4):
            if (l + d) % N == 0:
                continue
            row = 1536 if d == 4 else 512 + d * W
            put(l, d, src[row : row + W, :])
    for d in (0, 1):
        put(4, d, m4[512 + d * W : 512 + (d + 1) * W, :])
        put(4, d + 2, p4[d * W : (d + 1) * W, :])


def combine_kernel(
    s, x_own, aia, aib, adda, addb, vec_i, vec_j, x_far, msg, m1, m2, m3, p1, p2, p3, m4, p4,
    out1, out2, x_other, a_full, r, t, base, vecs, sems,
):
    role = s[0]
    q = s[1]
    terms = 2**NS - 1
    far_copy = pltpu.make_async_copy(x_far, x_other, sems.at[0])
    far_copy.start()
    copies = []
    for l, src in ((0, msg), (1, m1), (2, m2), (3, m3), (7, p1), (6, p2), (5, p3)):
        for half in range(2):
            copies.append((src, 1024 * half, 512 * half, l))
    copies += [(m4, 0, 0, 4), (p4, 256, 512, 4)]
    copies = [
        pltpu.make_async_copy(
            src.at[pl.ds(first, 512)],
            a_full.at[pl.ds(to, 512), pl.ds(l * W, W)],
            sems.at[1 + i],
        )
        for i, (src, first, to, l) in enumerate(copies)
    ]
    for c in copies:
        c.start()
    vi = vec_i[...].astype(f32)
    vj = vec_j[...].astype(f32)

    def rotated_move(dst, row):
        def put(src):
            for l in range(N):
                dst[row : row + W, l * W : (l + 1) * W] = src[blk((q + l) % N), :].T

        pl.when(s[2] == 0)(lambda: put(aia))
        pl.when(s[2] == 1)(lambda: put(aib))

    def rotated_vector(rows, first):
        vecs[...] = rows
        return jnp.concatenate([vecs[pl.ds(first + (q + l) % N, 1), :] for l in range(N)], axis=1)

    def as_rows(vector):
        return jnp.broadcast_to(vector, (16, D)).astype(bf16)

    @pl.when(role == 0)
    def _():
        cov, info = x_own, x_other
        rotated_move(base, W)
        eta = rotated_vector(vj, N)
        w = rotated_vector(vi, 0)
        for c in copies:
            c.wait()
        r[0:W, :] = a_full[blk(q), :]
        r[W : W + 16, :] = as_rows(eta)
        out = dot(r[0 : W + 16, :], cov[...])
        base[0:W, :] = out[0:W].astype(bf16)
        w = w + out[W : W + 1]
        r[0 : 2 * W, :] = base[...]
        r[2 * W : 2 * W + 16, :] = as_rows(w)
        far_copy.wait()
        for _ in range(terms):
            t[...] = dot(r[...], info[...]).astype(bf16)
            out = dot(t[...], cov[...])
            r[0 : 2 * W, :] = (base[...].astype(f32) - out[0 : 2 * W]).astype(bf16)
            r[2 * W : 2 * W + 16, :] = as_rows(w - out[2 * W : 2 * W + 1])
        res = lax.dot_general(
            r[...], a_full[...], (((1,), (1,)), ((), ())), preferred_element_type=f32
        )

        def put_c(src):
            for l in range(N):
                rows = slice(l * W, (l + 1) * W)
                out1[rows, :] = (res[0:W, rows].T + src[rows, :].astype(f32)).astype(bf16)
                out2[rows, :] = res[W : 2 * W, rows].astype(bf16).T

        pl.when(s[3] == 0)(lambda: put_c(adda))
        pl.when(s[3] == 1)(lambda: put_c(addb))
        rows = [
            res[2 * W : 2 * W + 1, l * W : (l + 1) * W] + vj[l : l + 1, :] for l in range(N)
        ]
        rows = rows + [jnp.zeros((1, W), f32)] * N
        out2[D : D + 2 * N, :] = jnp.concatenate(rows, axis=0).astype(bf16)

    @pl.when(role == 1)
    def _():
        info, cov = x_own, x_other
        top = slice(0, W)
        low = slice(W, W + 16)
        both = slice(0, W + 16)
        rotated_move(base, 0)
        r[top, :] = base[top, :]
        r[low, :] = as_rows(rotated_vector(vi, 0))
        eta = rotated_vector(vj, N)
        out = dot(r[both, :], info[...])
        start = eta - out[W : W + 1]
        t[top, :] = out[top].astype(bf16)
        t[low, :] = as_rows(start)
        far_copy.wait()
        for _ in range(terms):
            out = dot(t[both, :], cov[...])
            r[top, :] = (base[top, :].astype(f32) - out[top]).astype(bf16)
            r[low, :] = out[low].astype(bf16)
            out = dot(r[both, :], info[...])
            t[top, :] = out[top].astype(bf16)
            t[low, :] = as_rows(start - out[W : W + 1])
        for c in copies:
            c.wait()
        for l in range(N):
            x_other[blk((q + l) % N), 0 : W + 16] = t[both, l * W : (l + 1) * W].T
        for l in range(N):
            r[both, l * W : (l + 1) * W] = x_other[l * W : (l + 1) * W, 0 : W + 16].T
        res = dot(r[both, :], a_full[...])

        def put_j(src):
            for l in range(N):
                rows = blk((q + l) % N)
                out1[rows, :] = (
                    res[top, l * W : (l + 1) * W].T + src[rows, :].astype(f32)
                ).astype(bf16)

        pl.when(s[3] == 0)(lambda: put_j(adda))
        pl.when(s[3] == 1)(lambda: put_j(addb))
        vecs[...] = vi
        for l in range(N):
            spot = pl.ds(N + (q + l) % N, 1)
            vecs[spot, :] = vecs[spot, :] + res[W : W + 1, l * W : (l + 1) * W]
        rows = lax.broadcasted_iota(jnp.int32, (2 * N, W), 0)
        out2[0:D, :] = jnp.zeros((D, W), bf16)
        out2[D : D + 2 * N, :] = jnp.where(rows < N, 0.0, vecs[...]).astype(bf16)


def pick_kernel(s, cov, move, info, got, msg, sem):
    def copy(src):
        c = pltpu.make_async_copy(src.at[pl.ds(0, D)], msg.at[pl.ds(0, D)], sem.at[0])
        c.start()
        c.wait()

    pl.when(s[0] == 0)(lambda: copy(cov))
    pl.when(s[0] == 1)(lambda: copy(move))
    pl.when(s[0] == 2)(lambda: copy(info))
    pl.when(s[0] == 3)(lambda: copy(got))


def finish_kernel(s, vec_own, vec_got, own1, own2, got1, got2, drift, belief, move, spread, weight, sems):
    def put(first, moved, last, b, e):
        copies = [
            pltpu.make_async_copy(first.at[pl.ds(0, D)], spread, sems.at[0]),
            pltpu.make_async_copy(moved.at[pl.ds(0, D)], move, sems.at[1]),
            pltpu.make_async_copy(last.at[pl.ds(0, D)], weight, sems.at[2]),
        ]
        for c in copies:
            c.start()
        b = b[...].astype(f32)
        e = e[...].astype(f32)
        for l in range(N):
            drift[:, l * W : (l + 1) * W] = b[l : l + 1, :].astype(bf16)
            belief[:, l * W : (l + 1) * W] = e[N + l : N + l + 1, :].astype(bf16)
        for c in copies:
            c.wait()

    pl.when(s[0] == 0)(lambda: put(own1, own2, got1, vec_own, vec_got))
    pl.when(s[0] == 1)(lambda: put(got1, got2, own1, vec_got, vec_own))


def swap(x, axis_bit):
    return lax.ppermute(x, "tm", [(i, i ^ (1 << axis_bit)) for i in range(lax.axis_size("tm"))])


def shift(x, by):
    return lax.ppermute(x, "panel", [(i, (i + by) % N) for i in range(N)])


def ring(msg, side):
    ups, downs = [shift(msg, 1)], [shift(msg, -1)]
    extra = side()
    first, second, extra = lax.optimization_barrier((ups[0], downs[0], extra))
    ups, downs = [first], [second]
    for _ in range(2):
        ups.append(shift(ups[-1], 1))
        downs.append(shift(downs[-1], -1))
    m4 = shift(downs[-1][0:HALF], -1)
    p4 = shift(ups[-1][HALF : 2 * HALF], 1)
    return downs + ups + [m4, p4], extra


def combined(role, q, x_pair, x_pick, ring_pair, ring_pick, side):
    ring_scalars = jnp.stack([role, q, x_pick, ring_pick])
    (msg,) = call(
        ring_kernel,
        [struct(RING, W)],
        (pltpu.SemaphoreType.DMA((7,)),),
        ring_scalars,
        *x_pair,
        *ring_pair,
        vmem=0,
        vmem_out=False,
    )
    parts, (ai_pair, ai_pick, add_pair, add_pick, vec_i, vec_j) = ring(msg, side)
    (x_full,) = call(assemble_kernel, [struct(D, D)], (), ring_scalars, *x_pair, *parts)
    x_far = swap(x_full, 0)
    return call(
        combine_kernel,
        [struct(D, W), struct(D + 2 * N, W)],
        (
            pltpu.VMEM((D, D), bf16),
            pltpu.VMEM((D, D), bf16),
            pltpu.VMEM((2 * W + 16, D), bf16),
            pltpu.VMEM((2 * W + 16, D), bf16),
            pltpu.VMEM((2 * W, D), bf16),
            pltpu.VMEM((2 * N, W), f32),
            pltpu.SemaphoreType.DMA((17,)),
        ),
        jnp.stack([role, q, ai_pick, add_pick]),
        x_full,
        *ai_pair,
        *add_pair,
        vec_i,
        vec_j,
        x_far,
        msg,
        *parts,
        vmem=7,
    )


def local(transition, drift, spread, belief, precision, probe_hosts, probe_values):
    q = lax.axis_index("panel").astype(jnp.int32)
    t = lax.axis_index("tm").astype(jnp.int32)
    role = t & 1
    odd = (t >> 1) & 1
    zero = jnp.zeros((), jnp.int32)
    move, cov, info = transition[0], spread[0], precision[0]
    got_move = swap(move, 0)

    def side0():
        first, own_vec = call(
            start_kernel,
            [struct(D + 2 * N, W), struct(2 * N, W)],
            (),
            jnp.stack([role, q]),
            cov,
            info,
            drift,
            belief,
            probe_hosts.reshape(-1, 1),
            probe_values.reshape(-1, 1),
        )
        got = swap(first, 0)
        got_vec = got[D:]
        vec_i = jnp.where(role == 0, own_vec, got_vec)
        vec_j = jnp.where(role == 0, got_vec, own_vec)
        return (move, got_move), role, (got, got), zero, vec_i, vec_j

    out1, out2 = combined(role, q, (cov, info), role, (got_move, got_move), zero, side0)
    near = odd == 0
    got2 = swap(out2, 0)
    own_vec = out2[D:] + got2[D:]
    choice = jnp.where(role == 0, odd, 3 - odd)
    (panel,) = call(
        pick_kernel,
        [struct(D, W)],
        (pltpu.SemaphoreType.DMA((1,)),),
        choice[None],
        out1,
        out2,
        out1,
        got2,
        vmem=0,
        vmem_out=False,
    )
    far = swap(panel, 1)

    def side1():
        rest = jnp.where(role == 0, jnp.where(near, out2[:D], out1), out1)
        bundle = swap(jnp.concatenate([rest, own_vec], axis=0), 1)
        far_vec = bundle[D:]
        vec_i = jnp.where(near, own_vec, far_vec)
        vec_j = jnp.where(near, far_vec, own_vec)
        early_move = jnp.where(
            role == 0,
            jnp.where(near, out2[:D], bundle[:D]),
            jnp.where(near, got2[:D], far),
        )
        return (early_move, early_move), zero, (bundle, out1), role ^ odd, vec_i, vec_j

    ring_a = jnp.where(role == 0, 1 - odd, odd)
    local_move = jnp.where(role == 0, out2[:D], got2[:D])
    out1, out2 = combined(role, q, (out1, far), role ^ odd, (local_move, far), ring_a, side1)
    got1 = swap(out1, 0)
    got2 = swap(out2, 0)
    panel = struct(D, W)
    row = struct(1, D)
    drift, belief, move, cov, info = call(
        finish_kernel,
        [row, row, panel, panel, panel],
        (pltpu.SemaphoreType.DMA((3,)),),
        role[None],
        out2[D:],
        got2[D:],
        out1,
        out2,
        got1,
        got2,
        vmem=2,
        vmem_out=[True, True, False, False, False],
    )
    return move[None], drift, cov[None], belief, info[None]


def solution(mesh):
    in_specs = (
        P("tm", None, "panel"),
        P("tm", None),
        P("tm", None, "panel"),
        P("tm", None),
        P("tm", None, "panel"),
        P("tm", None),
        P("tm", None),
    )
    out_specs = (
        P("tm", None, "panel"),
        P("tm", None),
        P("tm", None, "panel"),
        P("tm", None),
        P("tm", None, "panel"),
    )
    return jax.shard_map(local, mesh=mesh, in_specs=in_specs, out_specs=out_specs, check_vma=False)
```

```python
import jax
import jax.numpy as jnp
from jax import lax
from jax.experimental import pallas as pl
from jax.experimental.pallas import tpu as pltpu
from jax.sharding import PartitionSpec as P


NS = 2
W = 128
N = 8
D = W * N
RING = 1664
HALF = 768
INTERPRET = False

f32 = jnp.float32
bf16 = jnp.bfloat16


def dot(a, b):
    return jnp.dot(a, b, preferred_element_type=f32)


def call(kernel, out_shape, scratch, scalars, *args, vmem=None):
    vm = pl.BlockSpec(memory_space=pltpu.VMEM)
    hbm = pl.BlockSpec(memory_space=pl.ANY)
    staged = len(args) if vmem is None else vmem
    return pl.pallas_call(
        kernel,
        out_shape=list(out_shape),
        in_specs=[pl.BlockSpec(memory_space=pltpu.SMEM)]
        + [vm] * staged
        + [hbm] * (len(args) - staged),
        out_specs=[vm] * len(out_shape),
        scratch_shapes=list(scratch),
        compiler_params=pltpu.CompilerParams(vmem_limit_bytes=56 * 2**20),
        interpret=INTERPRET,
    )(scalars, *args)


def struct(*shape):
    return jax.ShapeDtypeStruct(shape, bf16)


def blk(index):
    return pl.ds(pl.multiple_of(index * W, W), W)


def start_kernel(s, spread, weight, drift, belief, hosts, values, msg, own_vec):
    role = s[0]

    @pl.when(role == 0)
    def _():
        msg[0:D, :] = weight[...]

    @pl.when(role == 1)
    def _():
        msg[0:D, :] = spread[...]

    eye = lax.broadcasted_iota(jnp.int32, (W, W), 0) == lax.broadcasted_iota(jnp.int32, (W, W), 1)

    def column(row):
        return jnp.sum(jnp.where(eye, row, 0.0), axis=1, keepdims=True)

    lane = lax.broadcasted_iota(jnp.int32, (W, W), 1).astype(f32)
    sums = [jnp.zeros((1, W), f32)] * N
    for c in range(hosts.shape[1] // W):
        part = slice(c * W, (c + 1) * W)
        spot = column(2.0 * hosts[:, part].astype(f32))
        value = column(values[:, part])
        for k in range(N):
            hit = jnp.where(spot == lane + k * W, value, 0.0)
            sums[k] = sums[k] + jnp.sum(hit, axis=0, keepdims=True)
    eta = belief[...].astype(f32) + jnp.concatenate(sums, axis=1)
    eta = eta.astype(bf16).astype(f32)
    b = drift[...].astype(f32)
    rows = [b[:, k * W : (k + 1) * W] for k in range(N)] + [
        eta[:, k * W : (k + 1) * W] for k in range(N)
    ]
    vec = jnp.concatenate(rows, axis=0).astype(bf16)
    msg[D : D + 2 * N, :] = vec
    own_vec[...] = vec


def run_copies(copies):
    for c in copies:
        c.start()
    for c in copies:
        c.wait()


def ring_kernel(s, xa, xb, aa, ab, msg, sems):
    q = s[1]

    def x_copies(src):
        out = [
            pltpu.make_async_copy(src.at[blk((q + d) % N)], msg.at[pl.ds(512 + d * W, W)], sems.at[d])
            for d in range(4)
        ]
        return out + [
            pltpu.make_async_copy(src.at[blk((q + 4) % N)], msg.at[pl.ds(1536, W)], sems.at[4])
        ]

    def a_copies(src):
        return [
            pltpu.make_async_copy(src.at[pl.ds(0, 512)], msg.at[pl.ds(0, 512)], sems.at[5]),
            pltpu.make_async_copy(src.at[pl.ds(512, 512)], msg.at[pl.ds(1024, 512)], sems.at[6]),
        ]

    for i, x in ((0, xa), (1, xb)):
        for j, a in ((0, aa), (1, ab)):
            pl.when((s[2] == i) & (s[3] == j))(lambda x=x, a=a: run_copies(x_copies(x) + a_copies(a)))


def assemble_kernel(s, xa, xb, m1, m2, m3, p1, p2, p3, x_out):
    q = s[1]

    def put(l, d, block):
        r = (l + d) % N
        x_out[r * W : (r + 1) * W, l * W : (l + 1) * W] = block
        if d:
            x_out[l * W : (l + 1) * W, r * W : (r + 1) * W] = block.T

    def own(src):
        for d in range(N):
            put(0, d, src[blk((q + d) % N), :])

    pl.when(s[2] == 0)(lambda: own(xa))
    pl.when(s[2] == 1)(lambda: own(xb))
    for l, src in ((1, m1), (2, m2), (3, m3), (7, p1), (6, p2), (5, p3)):
        for d in range(5 if l < 4 else 4):
            if (l + d) % N == 0:
                continue
            row = 1536 if d == 4 else 512 + d * W
            put(l, d, src[row : row + W, :])
    x_out[4 * W :, 4 * W : 5 * W] = jnp.zeros((4 * W, W), bf16)
    x_out[4 * W : 5 * W, 5 * W :] = jnp.zeros((W, 3 * W), bf16)


def patch(dst, last):
    for d in range(4):
        block = last[d * W : (d + 1) * W, :]
        dst[(4 + d) * W : (5 + d) * W, 4 * W : 5 * W] = block
        if d:
            dst[4 * W : 5 * W, (4 + d) * W : (5 + d) * W] = block.T


def combine_kernel(
    s, last_own, last_far, aia, aib, adda, addb, vec_i, vec_j, x_here, x_far,
    msg, m1, m2, m3, p1, p2, p3, m4, p4,
    out1, out2, x_own, x_other, a_full, r, t, base, vecs, sems,
):
    role = s[0]
    q = s[1]
    terms = 2**NS - 1
    own_copy = pltpu.make_async_copy(x_here, x_own, sems.at[17])
    own_copy.start()
    copies = []
    for l, src in ((0, msg), (1, m1), (2, m2), (3, m3), (7, p1), (6, p2), (5, p3)):
        for half in range(2):
            copies.append((src, 1024 * half, 512 * half, l))
    copies += [(m4, 0, 0, 4), (p4, 256, 512, 4)]
    copies = [
        pltpu.make_async_copy(
            src.at[pl.ds(first, 512)],
            a_full.at[pl.ds(to, 512), pl.ds(l * W, W)],
            sems.at[1 + i],
        )
        for i, (src, first, to, l) in enumerate(copies)
    ]
    for c in copies:
        c.start()
    far_copy = pltpu.make_async_copy(x_far, x_other, sems.at[0])
    far_copy.start()
    vi = vec_i[...].astype(f32)
    vj = vec_j[...].astype(f32)

    def rotated_move(dst, row):
        def put(src):
            for l in range(N):
                dst[row : row + W, l * W : (l + 1) * W] = src[blk((q + l) % N), :].T

        pl.when(s[2] == 0)(lambda: put(aia))
        pl.when(s[2] == 1)(lambda: put(aib))

    def rotated_vector(rows, first):
        vecs[...] = rows
        return jnp.concatenate([vecs[pl.ds(first + (q + l) % N, 1), :] for l in range(N)], axis=1)

    def as_rows(vector):
        return jnp.broadcast_to(vector, (16, D)).astype(bf16)

    @pl.when(role == 0)
    def _():
        cov, info = x_own, x_other
        rotated_move(base, W)
        eta = rotated_vector(vj, N)
        w = rotated_vector(vi, 0)
        for c in copies:
            c.wait()
        r[0:W, :] = a_full[blk(q), :]
        own_copy.wait()
        patch(x_own, last_own)
        r[W : W + 16, :] = as_rows(eta)
        out = dot(r[0 : W + 16, :], cov[...])
        base[0:W, :] = out[0:W].astype(bf16)
        w = w + out[W : W + 1]
        r[0 : 2 * W, :] = base[...]
        r[2 * W : 2 * W + 16, :] = as_rows(w)
        far_copy.wait()
        patch(x_other, last_far)
        for _ in range(terms):
            t[...] = dot(r[...], info[...]).astype(bf16)
            out = dot(t[...], cov[...])
            r[0 : 2 * W, :] = (base[...].astype(f32) - out[0 : 2 * W]).astype(bf16)
            r[2 * W : 2 * W + 16, :] = as_rows(w - out[2 * W : 2 * W + 1])
        res = lax.dot_general(
            r[...], a_full[...], (((1,), (1,)), ((), ())), preferred_element_type=f32
        )

        def put_c(src):
            for l in range(N):
                rows = slice(l * W, (l + 1) * W)
                out1[rows, :] = (res[0:W, rows].T + src[rows, :].astype(f32)).astype(bf16)
                out2[rows, :] = res[W : 2 * W, rows].astype(bf16).T

        pl.when(s[3] == 0)(lambda: put_c(adda))
        pl.when(s[3] == 1)(lambda: put_c(addb))
        rows = [
            res[2 * W : 2 * W + 1, l * W : (l + 1) * W] + vj[l : l + 1, :] for l in range(N)
        ]
        rows = rows + [jnp.zeros((1, W), f32)] * N
        out2[D : D + 2 * N, :] = jnp.concatenate(rows, axis=0).astype(bf16)

    @pl.when(role == 1)
    def _():
        info, cov = x_own, x_other
        top = slice(0, W)
        low = slice(W, W + 16)
        both = slice(0, W + 16)
        rotated_move(base, 0)
        r[top, :] = base[top, :]
        r[low, :] = as_rows(rotated_vector(vi, 0))
        eta = rotated_vector(vj, N)
        own_copy.wait()
        patch(x_own, last_own)
        out = dot(r[both, :], info[...])
        start = eta - out[W : W + 1]
        t[top, :] = out[top].astype(bf16)
        t[low, :] = as_rows(start)
        far_copy.wait()
        patch(x_other, last_far)
        for _ in range(terms):
            out = dot(t[both, :], cov[...])
            r[top, :] = (base[top, :].astype(f32) - out[top]).astype(bf16)
            r[low, :] = out[low].astype(bf16)
            out = dot(r[both, :], info[...])
            t[top, :] = out[top].astype(bf16)
            t[low, :] = as_rows(start - out[W : W + 1])
        for c in copies:
            c.wait()
        for l in range(N):
            x_other[blk((q + l) % N), 0 : W + 16] = t[both, l * W : (l + 1) * W].T
        for l in range(N):
            r[both, l * W : (l + 1) * W] = x_other[l * W : (l + 1) * W, 0 : W + 16].T
        res = dot(r[both, :], a_full[...])

        def put_j(src):
            for l in range(N):
                rows = blk((q + l) % N)
                out1[rows, :] = (
                    res[top, l * W : (l + 1) * W].T + src[rows, :].astype(f32)
                ).astype(bf16)

        pl.when(s[3] == 0)(lambda: put_j(adda))
        pl.when(s[3] == 1)(lambda: put_j(addb))
        vecs[...] = vi
        for l in range(N):
            spot = pl.ds(N + (q + l) % N, 1)
            vecs[spot, :] = vecs[spot, :] + res[W : W + 1, l * W : (l + 1) * W]
        rows = lax.broadcasted_iota(jnp.int32, (2 * N, W), 0)
        out2[0:D, :] = jnp.zeros((D, W), bf16)
        out2[D : D + 2 * N, :] = jnp.where(rows < N, 0.0, vecs[...]).astype(bf16)


def pick_kernel(s, cov, move, info, got, msg, sem):
    def copy(src):
        c = pltpu.make_async_copy(src.at[pl.ds(0, D)], msg.at[pl.ds(0, D)], sem.at[0])
        c.start()
        c.wait()

    pl.when(s[0] == 0)(lambda: copy(cov))
    pl.when(s[0] == 1)(lambda: copy(move))
    pl.when(s[0] == 2)(lambda: copy(info))
    pl.when(s[0] == 3)(lambda: copy(got))


def finish_kernel(s, vec_own, vec_got, own1, own2, got1, got2, drift, belief, move, spread, weight, sems):
    def put(first, moved, last, b, e):
        copies = [
            pltpu.make_async_copy(first.at[pl.ds(0, D)], spread, sems.at[0]),
            pltpu.make_async_copy(moved.at[pl.ds(0, D)], move, sems.at[1]),
            pltpu.make_async_copy(last.at[pl.ds(0, D)], weight, sems.at[2]),
        ]
        for c in copies:
            c.start()
        b = b[...].astype(f32)
        e = e[...].astype(f32)
        for l in range(N):
            drift[:, l * W : (l + 1) * W] = b[l : l + 1, :].astype(bf16)
            belief[:, l * W : (l + 1) * W] = e[N + l : N + l + 1, :].astype(bf16)
        for c in copies:
            c.wait()

    pl.when(s[0] == 0)(lambda: put(own1, own2, got1, vec_own, vec_got))
    pl.when(s[0] == 1)(lambda: put(got1, got2, own1, vec_got, vec_own))


def swap(x, axis_bit):
    return lax.ppermute(x, "tm", [(i, i ^ (1 << axis_bit)) for i in range(lax.axis_size("tm"))])


def shift(x, by):
    return lax.ppermute(x, "panel", [(i, (i + by) % N) for i in range(N)])


def combined(role, q, x_pair, x_pick, ring_pair, ring_pick, gate, side):
    ring_scalars = jnp.stack([role, q, x_pick, ring_pick])
    (msg,) = call(
        ring_kernel,
        [struct(RING, W)],
        (pltpu.SemaphoreType.DMA((7,)),),
        ring_scalars,
        *x_pair,
        *ring_pair,
        vmem=0,
    )
    msg, gate = lax.optimization_barrier((msg, gate))
    p1 = shift(msg, 1)
    m1 = shift(msg, -1)
    p1, m1, extra = lax.optimization_barrier((p1, m1, side(gate)))
    ai_pair, ai_pick, add_pair, add_pick, vec_i, vec_j = extra
    p2, m2 = shift(p1, 1), shift(m1, -1)
    p3, m3 = shift(p2, 1), shift(m2, -1)
    p4 = shift(p3[HALF : 2 * HALF], 1)
    m4 = shift(m3[0:HALF], -1)
    (x_here,) = call(
        assemble_kernel, [struct(D, D)], (), ring_scalars, *x_pair, m1, m2, m3, p1, p2, p3
    )
    x_far = swap(x_here, 0)
    last_own = jnp.concatenate([m4[512:768], p4[0:256]], axis=0)
    last_far = swap(last_own, 0)
    return call(
        combine_kernel,
        [struct(D, W), struct(D + 2 * N, W)],
        (
            pltpu.VMEM((D, D), bf16),
            pltpu.VMEM((D, D), bf16),
            pltpu.VMEM((D, D), bf16),
            pltpu.VMEM((2 * W + 16, D), bf16),
            pltpu.VMEM((2 * W + 16, D), bf16),
            pltpu.VMEM((2 * W, D), bf16),
            pltpu.VMEM((2 * N, W), f32),
            pltpu.SemaphoreType.DMA((18,)),
        ),
        jnp.stack([role, q, ai_pick, add_pick]),
        last_own,
        last_far,
        *ai_pair,
        *add_pair,
        vec_i,
        vec_j,
        x_here,
        x_far,
        msg,
        m1,
        m2,
        m3,
        p1,
        p2,
        p3,
        m4,
        p4,
        vmem=8,
    )


def local(transition, drift, spread, belief, precision, probe_hosts, probe_values):
    q = lax.axis_index("panel").astype(jnp.int32)
    t = lax.axis_index("tm").astype(jnp.int32)
    role = t & 1
    odd = (t >> 1) & 1
    zero = jnp.zeros((), jnp.int32)
    move, cov, info = transition[0], spread[0], precision[0]
    got_move = swap(move, 0)

    def side0(drift):
        first, own_vec = call(
            start_kernel,
            [struct(D + 2 * N, W), struct(2 * N, W)],
            (),
            jnp.stack([role, q]),
            cov,
            info,
            drift,
            belief,
            probe_hosts,
            probe_values,
        )
        got = swap(first, 0)
        got_vec = got[D:]
        vec_i = jnp.where(role == 0, own_vec, got_vec)
        vec_j = jnp.where(role == 0, got_vec, own_vec)
        return (move, got_move), role, (got, got), zero, vec_i, vec_j

    out1, out2 = combined(
        role, q, (cov, info), role, (got_move, got_move), zero, drift, side0
    )
    near = odd == 0
    got2 = swap(out2, 0)
    own_vec = out2[D:] + got2[D:]
    choice = jnp.where(role == 0, odd, 3 - odd)
    (panel,) = call(
        pick_kernel,
        [struct(D, W)],
        (pltpu.SemaphoreType.DMA((1,)),),
        choice[None],
        out1,
        out2,
        out1,
        got2,
        vmem=0,
    )
    far = swap(panel, 1)

    def side1(own_vec):
        rest = jnp.where(role == 0, jnp.where(near, out2[:D], out1), out1)
        bundle = swap(jnp.concatenate([rest, own_vec], axis=0), 1)
        far_vec = bundle[D:]
        vec_i = jnp.where(near, own_vec, far_vec)
        vec_j = jnp.where(near, far_vec, own_vec)
        early_move = jnp.where(
            role == 0,
            jnp.where(near, out2[:D], bundle[:D]),
            jnp.where(near, got2[:D], far),
        )
        return (early_move, early_move), zero, (bundle, out1), role ^ odd, vec_i, vec_j

    ring_a = jnp.where(role == 0, 1 - odd, odd)
    local_move = jnp.where(role == 0, out2[:D], got2[:D])
    out1, out2 = combined(
        role, q, (out1, far), role ^ odd, (local_move, far), ring_a, own_vec, side1
    )
    got1 = swap(out1, 0)
    got2 = swap(out2, 0)
    panel = struct(D, W)
    row = struct(1, D)
    drift, belief, move, cov, info = call(
        finish_kernel,
        [row, row, panel, panel, panel],
        (pltpu.SemaphoreType.DMA((3,)),),
        role[None],
        out2[D:],
        got2[D:],
        out1,
        out2,
        got1,
        got2,
        vmem=2,
    )
    return move[None], drift, cov[None], belief, info[None]


def solution(mesh):
    in_specs = (
        P("tm", None, "panel"),
        P("tm", None),
        P("tm", None, "panel"),
        P("tm", None),
        P("tm", None, "panel"),
        P("tm", None),
        P("tm", None),
    )
    out_specs = (
        P("tm", None, "panel"),
        P("tm", None),
        P("tm", None, "panel"),
        P("tm", None),
        P("tm", None, "panel"),
    )
    return jax.shard_map(local, mesh=mesh, in_specs=in_specs, out_specs=out_specs, check_vma=False)
```

```python
import functools

import jax
import jax.numpy as jnp
from jax import lax
from jax.experimental import pallas as pl
from jax.experimental.pallas import tpu as pltpu
from jax.sharding import PartitionSpec as P


NS = 2
W = 128
N = 8
D = W * N
RING = 1664
HALF = 768
INTERPRET = False

f32 = jnp.float32
bf16 = jnp.bfloat16


def dot(a, b):
    return jnp.dot(a, b, preferred_element_type=f32)


def call(kernel, out_shape, scratch, *args, vmem=None, vmem_out=True):
    vm = pl.BlockSpec(memory_space=pltpu.VMEM)
    hbm = pl.BlockSpec(memory_space=pl.ANY)
    staged = len(args) if vmem is None else vmem
    flags = vmem_out if isinstance(vmem_out, list) else [vmem_out] * len(out_shape)
    return pl.pallas_call(
        kernel,
        out_shape=list(out_shape),
        in_specs=[vm] * staged + [hbm] * (len(args) - staged),
        out_specs=[vm if flag else hbm for flag in flags],
        scratch_shapes=list(scratch),
        compiler_params=pltpu.CompilerParams(vmem_limit_bytes=56 * 2**20),
        interpret=INTERPRET,
    )(*args)


def place():
    t = lax.axis_index("tm").astype(jnp.int32)
    return t & 1, (t >> 1) & 1, lax.axis_index("panel").astype(jnp.int32)


def each_state(run):
    core, odd, _ = place()
    for i in (0, 1):
        for j in (0, 1):
            pl.when((core == i) & (odd == j))(lambda i=i, j=j: run(i, j))


def stream(pieces, buf, sems_in, sems_out):
    ins = [
        pltpu.make_async_copy(src.at[pl.ds(a, W)], buf.at[pl.ds(k * W, W)], sems_in.at[k])
        for k, (src, a, _, _) in enumerate(pieces)
    ]
    outs = [
        pltpu.make_async_copy(buf.at[pl.ds(k * W, W)], dst.at[pl.ds(b, W)], sems_out.at[k])
        for k, (_, _, dst, b) in enumerate(pieces)
    ]
    for c in ins:
        c.start()
    for c, o in zip(ins, outs):
        c.wait()
        o.start()
    for o in outs:
        o.wait()


def streaming(pieces):
    return (
        pltpu.VMEM((pieces * W, W), bf16),
        pltpu.SemaphoreType.DMA((pieces,)),
        pltpu.SemaphoreType.DMA((pieces,)),
    )


def struct(*shape):
    return jax.ShapeDtypeStruct(shape, bf16)


def at(index):
    return pl.multiple_of(index * W, W)


def blk(index):
    return pl.ds(at(index), W)


def start_kernel(move, drift, belief, hosts, values, msg, own_vec):
    msg[0:D, :] = move[...]
    eye = lax.broadcasted_iota(jnp.int32, (W, W), 0) == lax.broadcasted_iota(jnp.int32, (W, W), 1)

    def column(row):
        return jnp.sum(jnp.where(eye, row, 0.0), axis=1, keepdims=True)

    lane = lax.broadcasted_iota(jnp.int32, (W, W), 1).astype(f32)
    sums = [jnp.zeros((1, W), f32)] * N
    for c in range(hosts.shape[1] // W):
        part = slice(c * W, (c + 1) * W)
        spot = column(2.0 * hosts[:, part].astype(f32))
        value = column(values[:, part])
        for k in range(N):
            hit = jnp.where(spot == lane + k * W, value, 0.0)
            sums[k] = sums[k] + jnp.sum(hit, axis=0, keepdims=True)
    eta = belief[...].astype(f32) + jnp.concatenate(sums, axis=1)
    eta = eta.astype(bf16).astype(f32)
    b = drift[...].astype(f32)
    rows = [b[:, k * W : (k + 1) * W] for k in range(N)] + [
        eta[:, k * W : (k + 1) * W] for k in range(N)
    ]
    vec = jnp.concatenate(rows, axis=0).astype(bf16)
    msg[D : D + 2 * N, :] = vec
    own_vec[...] = vec


def ring_kernel(sources, *refs):
    *inputs, msg, buf, sems_in, sems_out = refs
    q = place()[2]

    def run(core, odd):
        x, a = (inputs[k] for k in sources(core, odd))
        pieces = [(x, at((q + d) % N), msg, 512 + d * W if d < 4 else 1536) for d in range(5)]
        pieces += [(a, k * W, msg, k * W if k < 4 else 512 + k * W) for k in range(N)]
        stream(pieces, buf, sems_in, sems_out)

    each_state(run)


def assemble_kernel(pick, xa, xb, m1, m2, m3, p1, p2, p3, x_out):
    core, odd, q = place()

    def put(l, d, block):
        r = (l + d) % N
        x_out[r * W : (r + 1) * W, l * W : (l + 1) * W] = block
        if d:
            x_out[l * W : (l + 1) * W, r * W : (r + 1) * W] = block.T

    def own(src):
        for d in range(N):
            put(0, d, src[blk((q + d) % N), :])

    pl.when(pick(core, odd) == 0)(lambda: own(xa))
    pl.when(pick(core, odd) == 1)(lambda: own(xb))
    for l, src in ((1, m1), (2, m2), (3, m3), (7, p1), (6, p2), (5, p3)):
        for d in range(5 if l < 4 else 4):
            if (l + d) % N == 0:
                continue
            row = 1536 if d == 4 else 512 + d * W
            put(l, d, src[row : row + W, :])
    x_out[4 * W :, 4 * W : 5 * W] = jnp.zeros((4 * W, W), bf16)
    x_out[4 * W : 5 * W, 5 * W :] = jnp.zeros((W, 3 * W), bf16)


def patch(dst, last):
    for d in range(4):
        block = last[d * W : (d + 1) * W, :]
        dst[(4 + d) * W : (5 + d) * W, 4 * W : 5 * W] = block
        if d:
            dst[4 * W : 5 * W, (4 + d) * W : (5 + d) * W] = block.T


def combine_kernel(own_is_cov, sides, count, last_own, last_far, vec_i, vec_j, *refs):
    side_refs = refs[:count]
    (x_here, x_far, msg, m1, m2, m3, p1, p2, p3, m4, p4, out1, out2,
     x_own, x_other, a_full, r, t, base, vecs, ai, add, sems) = refs[count:]
    core, _, q = place()
    terms = 2**NS - 1

    def whole(src, dst, first):
        return [
            pltpu.make_async_copy(
                src.at[pl.ds(k * 256, 256)], dst.at[pl.ds(k * 256, 256)], sems.at[first + k]
            )
            for k in range(4)
        ]

    own_copies = whole(x_here, x_own, 18)
    far_copies = whole(x_far, x_other, 22)
    copies = []
    for l, src in ((0, msg), (1, m1), (2, m2), (3, m3), (7, p1), (6, p2), (5, p3)):
        for half in range(2):
            copies.append((src, 1024 * half, 512 * half, l))
    copies += [(m4, 0, 0, 4), (p4, 256, 512, 4)]
    copies = [
        pltpu.make_async_copy(
            src.at[pl.ds(first, 512)], a_full.at[pl.ds(to, 512), pl.ds(l * W, W)], sems.at[2 + i]
        )
        for i, (src, first, to, l) in enumerate(copies)
    ]
    side_copies = [
        pltpu.make_async_copy(side_refs[0].at[pl.ds(0, D)], dst, sems.at[k])
        for k, dst in enumerate((ai, add))
    ]

    def start_sides(i, j):
        for k, dst in zip(sides(i, j), (ai, add)):
            sem = sems.at[0] if dst is ai else sems.at[1]
            pltpu.make_async_copy(side_refs[k].at[pl.ds(0, D)], dst, sem).start()

    each_state(start_sides)

    def start(group):
        for c in group:
            c.start()

    def wait(group):
        for c in group:
            c.wait()

    @pl.when(core == 1)
    def _():
        start(copies)
        start(own_copies if own_is_cov else far_copies)
        start(far_copies if own_is_cov else own_copies)

    @pl.when(core == 0)
    def _():
        start(own_copies if own_is_cov else far_copies)
        start(far_copies if own_is_cov else own_copies)
        start(copies)

    vi = vec_i[...].astype(f32)
    vj = vec_j[...].astype(f32)

    def ready_own():
        wait(own_copies)
        patch(x_own, last_own)

    def ready_far():
        wait(far_copies)
        patch(x_other, last_far)

    first_ready, then_ready = (ready_own, ready_far) if own_is_cov else (ready_far, ready_own)
    first_x, then_x = (x_own, x_other) if own_is_cov else (x_other, x_own)

    def rotated_move(dst, row):
        for l in range(N):
            dst[row : row + W, l * W : (l + 1) * W] = ai[blk((q + l) % N), :].T

    def rotated_vector(rows, first):
        vecs[...] = rows
        return jnp.concatenate([vecs[pl.ds(first + (q + l) % N, 1), :] for l in range(N)], axis=1)

    def as_rows(vector):
        return jnp.broadcast_to(vector, (16, D)).astype(bf16)

    @pl.when(core == 1)
    def _():
        cov, info = first_x, then_x
        eta = rotated_vector(vj, N)
        w = rotated_vector(vi, 0)
        side_copies[0].wait()
        rotated_move(base, W)
        r[W : W + 16, :] = as_rows(eta)
        wait(copies)
        r[0:W, :] = a_full[blk(q), :]
        first_ready()
        out = dot(r[0 : W + 16, :], cov[...])
        base[0:W, :] = out[0:W].astype(bf16)
        w = w + out[W : W + 1]
        r[0 : 2 * W, :] = base[...]
        r[2 * W : 2 * W + 16, :] = as_rows(w)
        then_ready()
        for _ in range(terms):
            t[...] = dot(r[...], info[...]).astype(bf16)
            out = dot(t[...], cov[...])
            r[0 : 2 * W, :] = (base[...].astype(f32) - out[0 : 2 * W]).astype(bf16)
            r[2 * W : 2 * W + 16, :] = as_rows(w - out[2 * W : 2 * W + 1])
        res = lax.dot_general(
            r[...], a_full[...], (((1,), (1,)), ((), ())), preferred_element_type=f32
        )
        side_copies[1].wait()
        for l in range(N):
            rows = slice(l * W, (l + 1) * W)
            out1[rows, :] = (res[0:W, rows].T + add[rows, :].astype(f32)).astype(bf16)
            out2[rows, :] = res[W : 2 * W, rows].astype(bf16).T
        rows = [res[2 * W : 2 * W + 1, l * W : (l + 1) * W] + vj[l : l + 1, :] for l in range(N)]
        rows = rows + [jnp.zeros((1, W), f32)] * N
        out2[D : D + 2 * N, :] = jnp.concatenate(rows, axis=0).astype(bf16)

    @pl.when(core == 0)
    def _():
        info, cov = first_x, then_x
        top = slice(0, W)
        low = slice(W, W + 16)
        both = slice(0, W + 16)
        eta = rotated_vector(vj, N)
        side_copies[0].wait()
        rotated_move(base, 0)
        r[top, :] = base[top, :]
        r[low, :] = as_rows(rotated_vector(vi, 0))
        first_ready()
        out = dot(r[both, :], info[...])
        start_vec = eta - out[W : W + 1]
        t[top, :] = out[top].astype(bf16)
        t[low, :] = as_rows(start_vec)
        then_ready()
        for _ in range(terms):
            out = dot(t[both, :], cov[...])
            r[top, :] = (base[top, :].astype(f32) - out[top]).astype(bf16)
            r[low, :] = out[low].astype(bf16)
            out = dot(r[both, :], info[...])
            t[top, :] = out[top].astype(bf16)
            t[low, :] = as_rows(start_vec - out[W : W + 1])
        wait(copies)
        side_copies[1].wait()
        for l in range(N):
            x_other[blk((q + l) % N), 0 : W + 16] = t[both, l * W : (l + 1) * W].T
        for l in range(N):
            r[both, l * W : (l + 1) * W] = x_other[l * W : (l + 1) * W, 0 : W + 16].T
        res = dot(r[both, :], a_full[...])
        for l in range(N):
            rows = blk((q + l) % N)
            out1[rows, :] = (res[top, l * W : (l + 1) * W].T + add[rows, :].astype(f32)).astype(bf16)
        vecs[...] = vi
        for l in range(N):
            spot = pl.ds(N + (q + l) % N, 1)
            vecs[spot, :] = vecs[spot, :] + res[W : W + 1, l * W : (l + 1) * W]
        rows = lax.broadcasted_iota(jnp.int32, (2 * N, W), 0)
        out2[0:D, :] = jnp.zeros((D, W), bf16)
        out2[D : D + 2 * N, :] = jnp.where(rows < N, 0.0, vecs[...]).astype(bf16)


def pick_kernel(out1, out2, got2, msg, buf, sems_in, sems_out):
    def run(core, odd):
        src = out2 if (core, odd) == (1, 1) else got2 if (core, odd) == (0, 0) else out1
        stream([(src, k * W, msg, k * W) for k in range(N)], buf, sems_in, sems_out)

    each_state(run)


def finish_kernel(
    own1, own2, got1, got2, drift, belief, move, spread, weight, buf, sems_in, sems_out, vec, sems
):
    core = place()[0]

    def put(first, moved, last, b, e):
        tails = [
            pltpu.make_async_copy(
                src.at[pl.ds(D, 2 * N)], vec.at[pl.ds(k * 2 * N, 2 * N)], sems.at[k]
            )
            for k, src in enumerate((b, e))
        ]
        for c in tails:
            c.start()
        pieces = []
        for src, dst in ((first, spread), (moved, move), (last, weight)):
            pieces += [(src, k * W, dst, k * W) for k in range(N)]
        stream(pieces, buf, sems_in, sems_out)
        for c in tails:
            c.wait()
        rows = vec[...].astype(f32)
        for l in range(N):
            drift[:, l * W : (l + 1) * W] = rows[l : l + 1, :].astype(bf16)
            belief[:, l * W : (l + 1) * W] = rows[3 * N + l : 3 * N + l + 1, :].astype(bf16)

    pl.when(core == 1)(lambda: put(own1, own2, got1, own2, got2))
    pl.when(core == 0)(lambda: put(got1, got2, own1, got2, own2))


def swap(x, axis_bit):
    return lax.ppermute(x, "tm", [(i, i ^ (1 << axis_bit)) for i in range(lax.axis_size("tm"))])


def shift(x, by):
    return lax.ppermute(x, "panel", [(i, (i + by) % N) for i in range(N)])


def combined(own_is_cov, x_pair, x_pick, ring_refs, sources, gate, side, sides):
    (msg,) = call(
        functools.partial(ring_kernel, sources),
        [struct(RING, W)],
        streaming(RING // W),
        *ring_refs,
        vmem=0,
        vmem_out=False,
    )
    msg, gate = lax.optimization_barrier((msg, gate))
    p1 = shift(msg, 1)
    m1 = shift(msg, -1)
    p1, m1, (vec_i, vec_j, side_refs) = lax.optimization_barrier((p1, m1, side(gate)))
    p2, m2 = shift(p1, 1), shift(m1, -1)
    p3, m3 = shift(p2, 1), shift(m2, -1)
    p4 = shift(p3[HALF : 2 * HALF], 1)
    m4 = shift(m3[0:HALF], -1)
    (x_here,) = call(
        functools.partial(assemble_kernel, x_pick),
        [struct(D, D)],
        (),
        *x_pair,
        m1,
        m2,
        m3,
        p1,
        p2,
        p3,
    )
    x_far = swap(x_here, 0)
    last_own = jnp.concatenate([m4[512:768], p4[0:256]], axis=0)
    last_far = swap(last_own, 0)
    return call(
        functools.partial(combine_kernel, own_is_cov, sides, len(side_refs)),
        [struct(D, W), struct(D + 2 * N, W)],
        (
            pltpu.VMEM((D, D), bf16),
            pltpu.VMEM((D, D), bf16),
            pltpu.VMEM((D, D), bf16),
            pltpu.VMEM((2 * W + 16, D), bf16),
            pltpu.VMEM((2 * W + 16, D), bf16),
            pltpu.VMEM((2 * W, D), bf16),
            pltpu.VMEM((2 * N, W), f32),
            pltpu.VMEM((D, W), bf16),
            pltpu.VMEM((D, W), bf16),
            pltpu.SemaphoreType.DMA((26,)),
        ),
        last_own,
        last_far,
        vec_i,
        vec_j,
        *side_refs,
        x_here,
        x_far,
        msg,
        m1,
        m2,
        m3,
        p1,
        p2,
        p3,
        m4,
        p4,
        vmem=4,
    )


def local(transition, drift, spread, belief, precision, probe_hosts, probe_values):
    core, odd, _ = place()
    near = odd == 0
    move, cov, info = transition[0], spread[0], precision[0]

    def side0(drift):
        first, own_vec = call(
            start_kernel,
            [struct(D + 2 * N, W), struct(2 * N, W)],
            (),
            move,
            drift,
            belief,
            probe_hosts,
            probe_values,
        )
        got = swap(first, 0)
        got_vec = got[D:]
        vec_i = jnp.where(core == 0, own_vec, got_vec)
        vec_j = jnp.where(core == 0, got_vec, own_vec)
        return vec_i, vec_j, (move, got, cov, info)

    out1, out2 = combined(
        False,
        (cov, info),
        lambda core, odd: core,
        (cov, info, move),
        lambda core, odd: (core, 2),
        drift,
        side0,
        lambda core, odd: (core, 3 - core),
    )
    got2 = swap(out2, 0)
    own_vec = out2[D:] + got2[D:]
    (panel,) = call(
        pick_kernel, [struct(D, W)], streaming(N), out1, out2, got2, vmem=0, vmem_out=False
    )
    far = swap(panel, 1)

    def side1(own_vec):
        rest = jnp.where((core == 1) & near, out2[:D], out1)
        bundle = swap(jnp.concatenate([rest, own_vec], axis=0), 1)
        far_vec = bundle[D:]
        vec_i = jnp.where(near, own_vec, far_vec)
        vec_j = jnp.where(near, far_vec, own_vec)
        return vec_i, vec_j, (out1, out2, got2, far, bundle)

    sources = {(1, 0): (0, 3), (1, 1): (3, 1), (0, 0): (3, 2), (0, 1): (0, 3)}
    sides = {(1, 0): (1, 4), (1, 1): (4, 0), (0, 0): (2, 0), (0, 1): (3, 4)}
    out1, out2 = combined(
        True,
        (out1, far),
        lambda core, odd: 1 ^ core ^ odd,
        (out1, out2, got2, far),
        lambda core, odd: sources[core, odd],
        own_vec,
        side1,
        lambda core, odd: sides[core, odd],
    )
    got1 = swap(out1, 0)
    got2 = swap(out2, 0)
    panel = struct(D, W)
    row = struct(1, D)
    drift, belief, move, cov, info = call(
        finish_kernel,
        [row, row, panel, panel, panel],
        streaming(3 * N) + (pltpu.VMEM((4 * N, W), bf16), pltpu.SemaphoreType.DMA((2,))),
        out1,
        out2,
        got1,
        got2,
        vmem=0,
        vmem_out=[True, True, False, False, False],
    )
    return move[None], drift, cov[None], belief, info[None]


def solution(mesh):
    in_specs = (
        P("tm", None, "panel"),
        P("tm", None),
        P("tm", None, "panel"),
        P("tm", None),
        P("tm", None, "panel"),
        P("tm", None),
        P("tm", None),
    )
    out_specs = (
        P("tm", None, "panel"),
        P("tm", None),
        P("tm", None, "panel"),
        P("tm", None),
        P("tm", None, "panel"),
    )
    return jax.shard_map(local, mesh=mesh, in_specs=in_specs, out_specs=out_specs, check_vma=False)
```

```python
import functools

import jax
import jax.numpy as jnp
from jax import lax
from jax.experimental import pallas as pl
from jax.experimental.pallas import tpu as pltpu
from jax.sharding import PartitionSpec as P


NS = 2
W = 128
N = 8
D = W * N
UP = 1536
DOWN = 1664
HALF = 768
INTERPRET = False

f32 = jnp.float32
bf16 = jnp.bfloat16


def dot(a, b):
    return jnp.dot(a, b, preferred_element_type=f32)


def call(kernel, out_shape, scratch, *args, vmem=None, vmem_out=True):
    vm = pl.BlockSpec(memory_space=pltpu.VMEM)
    hbm = pl.BlockSpec(memory_space=pl.ANY)
    staged = len(args) if vmem is None else vmem
    flags = vmem_out if isinstance(vmem_out, list) else [vmem_out] * len(out_shape)
    return pl.pallas_call(
        kernel,
        out_shape=list(out_shape),
        in_specs=[vm] * staged + [hbm] * (len(args) - staged),
        out_specs=[vm if flag else hbm for flag in flags],
        scratch_shapes=list(scratch),
        compiler_params=pltpu.CompilerParams(vmem_limit_bytes=56 * 2**20),
        interpret=INTERPRET,
    )(*args)


def place():
    t = lax.axis_index("tm").astype(jnp.int32)
    return t & 1, (t >> 1) & 1, lax.axis_index("panel").astype(jnp.int32)


def each_state(run):
    core, odd, _ = place()
    for i in (0, 1):
        for j in (0, 1):
            pl.when((core == i) & (odd == j))(lambda i=i, j=j: run(i, j))


def stream(pieces, buf, sems_in, sems_out):
    ins, outs = [], []
    for k, (src, a, targets) in enumerate(pieces):
        part = buf.at[pl.ds(k * W, W)]
        ins.append(pltpu.make_async_copy(src.at[pl.ds(a, W)], part, sems_in.at[k]))
        outs.append(
            [
                pltpu.make_async_copy(part, dst.at[pl.ds(b, W)], sems_out.at[2 * k + i])
                for i, (dst, b) in enumerate(targets)
            ]
        )
    for c in ins:
        c.start()
    for c, group in zip(ins, outs):
        c.wait()
        for o in group:
            o.start()
    for group in outs:
        for o in group:
            o.wait()


def streaming(pieces):
    return (
        pltpu.VMEM((pieces * W, W), bf16),
        pltpu.SemaphoreType.DMA((pieces,)),
        pltpu.SemaphoreType.DMA((2 * pieces,)),
    )


def struct(*shape):
    return jax.ShapeDtypeStruct(shape, bf16)


def at(index):
    return pl.multiple_of(index * W, W)


def blk(index):
    return pl.ds(at(index), W)


def start_kernel(move, drift, belief, hosts, values, msg, own_vec):
    msg[0:D, :] = move[...]
    eye = lax.broadcasted_iota(jnp.int32, (W, W), 0) == lax.broadcasted_iota(jnp.int32, (W, W), 1)

    def column(row):
        return jnp.sum(jnp.where(eye, row, 0.0), axis=1, keepdims=True)

    lane = lax.broadcasted_iota(jnp.int32, (W, W), 1).astype(f32)
    sums = [jnp.zeros((1, W), f32)] * N
    for c in range(hosts.shape[1] // W):
        part = slice(c * W, (c + 1) * W)
        spot = column(2.0 * hosts[:, part].astype(f32))
        value = column(values[:, part])
        for k in range(N):
            hit = jnp.where(spot == lane + k * W, value, 0.0)
            sums[k] = sums[k] + jnp.sum(hit, axis=0, keepdims=True)
    eta = belief[...].astype(f32) + jnp.concatenate(sums, axis=1)
    eta = eta.astype(bf16).astype(f32)
    b = drift[...].astype(f32)
    rows = [b[:, k * W : (k + 1) * W] for k in range(N)] + [
        eta[:, k * W : (k + 1) * W] for k in range(N)
    ]
    vec = jnp.concatenate(rows, axis=0).astype(bf16)
    msg[D : D + 2 * N, :] = vec
    own_vec[...] = vec


def ring_kernel(sources, *refs):
    *inputs, up, down, buf, sems_in, sems_out = refs
    q = place()[2]

    def run(core, odd):
        x, a = (inputs[k] for k in sources(core, odd))
        spots = [(a, k * W, k * W if k < 4 else 512 + k * W) for k in range(N)]
        spots += [(x, at((q + d) % N), 512 + d * W) for d in range(4)]
        pieces = [(src, row, [(down, to), (up, to)]) for src, row, to in spots]
        pieces += [(x, at((q + 4) % N), [(down, UP)])]
        stream(pieces, buf, sems_in, sems_out)

    each_state(run)


def assemble_kernel(pick, xa, xb, m1, m2, m3, p1, p2, p3, x_out):
    core, odd, q = place()

    def put(l, d, block):
        r = (l + d) % N
        x_out[r * W : (r + 1) * W, l * W : (l + 1) * W] = block
        if d:
            x_out[l * W : (l + 1) * W, r * W : (r + 1) * W] = block.T

    def own(src):
        for d in range(N):
            put(0, d, src[blk((q + d) % N), :])

    pl.when(pick(core, odd) == 0)(lambda: own(xa))
    pl.when(pick(core, odd) == 1)(lambda: own(xb))
    for l, src in ((1, m1), (2, m2), (3, m3), (7, p1), (6, p2), (5, p3)):
        for d in range(5 if l < 4 else 4):
            if (l + d) % N == 0:
                continue
            row = 1536 if d == 4 else 512 + d * W
            put(l, d, src[row : row + W, :])
    x_out[4 * W :, 4 * W : 5 * W] = jnp.zeros((4 * W, W), bf16)
    x_out[4 * W : 5 * W, 5 * W :] = jnp.zeros((W, 3 * W), bf16)


def patch(dst, last):
    for d in range(4):
        block = last[d * W : (d + 1) * W, :]
        dst[(4 + d) * W : (5 + d) * W, 4 * W : 5 * W] = block
        if d:
            dst[4 * W : 5 * W, (4 + d) * W : (5 + d) * W] = block.T


def combine_kernel(own_is_cov, sides, count, last_own, last_far, vec_i, vec_j, *refs):
    side_refs = refs[:count]
    joined = len(refs) == count + 22
    if joined:
        out1 = refs[count + 11].at[pl.ds(0, D)]
        out2 = refs[count + 11].at[pl.ds(D, D + 2 * N)]
        refs = refs[: count + 11] + (out1, out2) + refs[count + 12 :]
    (x_here, x_far, msg, m1, m2, m3, p1, p2, p3, m4, p4, out1, out2,
     x_own, x_other, a_full, r, t, base, vecs, ai, add, sems) = refs[count:]
    core, _, q = place()
    terms = 2**NS - 1

    def whole(src, dst, first):
        return [
            pltpu.make_async_copy(
                src.at[pl.ds(k * 256, 256)], dst.at[pl.ds(k * 256, 256)], sems.at[first + k]
            )
            for k in range(4)
        ]

    own_copies = whole(x_here, x_own, 18)
    far_copies = whole(x_far, x_other, 22)
    copies = []
    for l, src in ((0, msg), (1, m1), (2, m2), (3, m3), (7, p1), (6, p2), (5, p3)):
        for half in range(2):
            copies.append((src, 1024 * half, 512 * half, l))
    copies += [(m4, 0, 0, 4), (p4, 256, 512, 4)]
    copies = [
        pltpu.make_async_copy(
            src.at[pl.ds(first, 512)], a_full.at[pl.ds(to, 512), pl.ds(l * W, W)], sems.at[2 + i]
        )
        for i, (src, first, to, l) in enumerate(copies)
    ]
    side_copies = [
        pltpu.make_async_copy(side_refs[0].at[pl.ds(0, D)], dst, sems.at[k])
        for k, dst in enumerate((ai, add))
    ]

    def start_sides(i, j):
        for k, dst in zip(sides(i, j), (ai, add)):
            sem = sems.at[0] if dst is ai else sems.at[1]
            pltpu.make_async_copy(side_refs[k].at[pl.ds(0, D)], dst, sem).start()

    each_state(start_sides)

    def start(group):
        for c in group:
            c.start()

    def wait(group):
        for c in group:
            c.wait()

    @pl.when(core == 1)
    def _():
        start(copies)
        start(own_copies if own_is_cov else far_copies)
        start(far_copies if own_is_cov else own_copies)

    @pl.when(core == 0)
    def _():
        start(own_copies if own_is_cov else far_copies)
        start(far_copies if own_is_cov else own_copies)
        start(copies)

    vi = vec_i[...].astype(f32)
    vj = vec_j[...].astype(f32)

    def ready_own():
        wait(own_copies)
        patch(x_own, last_own)

    def ready_far():
        wait(far_copies)
        patch(x_other, last_far)

    first_ready, then_ready = (ready_own, ready_far) if own_is_cov else (ready_far, ready_own)
    first_x, then_x = (x_own, x_other) if own_is_cov else (x_other, x_own)

    def rotated_move(dst, row):
        for l in range(N):
            dst[row : row + W, l * W : (l + 1) * W] = ai[blk((q + l) % N), :].T

    def rotated_vector(rows, first):
        vecs[...] = rows
        return jnp.concatenate([vecs[pl.ds(first + (q + l) % N, 1), :] for l in range(N)], axis=1)

    def as_rows(vector):
        return jnp.broadcast_to(vector, (16, D)).astype(bf16)

    @pl.when(core == 1)
    def _():
        cov, info = first_x, then_x
        eta = rotated_vector(vj, N)
        w = rotated_vector(vi, 0)
        side_copies[0].wait()
        rotated_move(base, W)
        r[W : W + 16, :] = as_rows(eta)
        wait(copies)
        r[0:W, :] = a_full[blk(q), :]
        first_ready()
        out = dot(r[0 : W + 16, :], cov[...])
        base[0:W, :] = out[0:W].astype(bf16)
        w = w + out[W : W + 1]
        r[0 : 2 * W, :] = base[...]
        r[2 * W : 2 * W + 16, :] = as_rows(w)
        then_ready()
        for _ in range(terms):
            t[...] = dot(r[...], info[...]).astype(bf16)
            out = dot(t[...], cov[...])
            r[0 : 2 * W, :] = (base[...].astype(f32) - out[0 : 2 * W]).astype(bf16)
            r[2 * W : 2 * W + 16, :] = as_rows(w - out[2 * W : 2 * W + 1])
        res = lax.dot_general(
            r[...], a_full[...], (((1,), (1,)), ((), ())), preferred_element_type=f32
        )
        side_copies[1].wait()
        for l in range(N):
            rows = slice(l * W, (l + 1) * W)
            out1[rows, :] = (res[0:W, rows].T + add[rows, :].astype(f32)).astype(bf16)
            out2[rows, :] = res[W : 2 * W, rows].astype(bf16).T
        rows = [res[2 * W : 2 * W + 1, l * W : (l + 1) * W] + vj[l : l + 1, :] for l in range(N)]
        rows = rows + [jnp.zeros((1, W), f32)] * N
        out2[D : D + 2 * N, :] = jnp.concatenate(rows, axis=0).astype(bf16)

    @pl.when(core == 0)
    def _():
        info, cov = first_x, then_x
        top = slice(0, W)
        low = slice(W, W + 16)
        both = slice(0, W + 16)
        eta = rotated_vector(vj, N)
        side_copies[0].wait()
        rotated_move(base, 0)
        r[top, :] = base[top, :]
        r[low, :] = as_rows(rotated_vector(vi, 0))
        first_ready()
        out = dot(r[both, :], info[...])
        start_vec = eta - out[W : W + 1]
        t[top, :] = out[top].astype(bf16)
        t[low, :] = as_rows(start_vec)
        then_ready()
        for _ in range(terms):
            out = dot(t[both, :], cov[...])
            r[top, :] = (base[top, :].astype(f32) - out[top]).astype(bf16)
            r[low, :] = out[low].astype(bf16)
            out = dot(r[both, :], info[...])
            t[top, :] = out[top].astype(bf16)
            t[low, :] = as_rows(start_vec - out[W : W + 1])
        wait(copies)
        side_copies[1].wait()
        for l in range(N):
            x_other[blk((q + l) % N), 0 : W + 16] = t[both, l * W : (l + 1) * W].T
        for l in range(N):
            r[both, l * W : (l + 1) * W] = x_other[l * W : (l + 1) * W, 0 : W + 16].T
        res = dot(r[both, :], a_full[...])
        for l in range(N):
            rows = blk((q + l) % N)
            out1[rows, :] = (res[top, l * W : (l + 1) * W].T + add[rows, :].astype(f32)).astype(bf16)
        vecs[...] = vi
        for l in range(N):
            spot = pl.ds(N + (q + l) % N, 1)
            vecs[spot, :] = vecs[spot, :] + res[W : W + 1, l * W : (l + 1) * W]
        rows = lax.broadcasted_iota(jnp.int32, (2 * N, W), 0)
        out2[0:D, :] = jnp.zeros((D, W), bf16)
        out2[D : D + 2 * N, :] = jnp.where(rows < N, 0.0, vecs[...]).astype(bf16)


def finish_kernel(own, got, drift, belief, move, spread, weight, buf, sems_in, sems_out, vec, sems):
    core = place()[0]

    def put(early, late):
        tails = [
            pltpu.make_async_copy(
                src.at[pl.ds(2 * D, 2 * N)], vec.at[pl.ds(k * 2 * N, 2 * N)], sems.at[k]
            )
            for k, src in enumerate((early, late))
        ]
        for c in tails:
            c.start()
        pieces = []
        for src, first, dst in ((early, 0, spread), (early, D, move), (late, 0, weight)):
            pieces += [(src, first + k * W, [(dst, k * W)]) for k in range(N)]
        stream(pieces, buf, sems_in, sems_out)
        for c in tails:
            c.wait()
        rows = vec[...].astype(f32)
        for l in range(N):
            drift[:, l * W : (l + 1) * W] = rows[l : l + 1, :].astype(bf16)
            belief[:, l * W : (l + 1) * W] = rows[3 * N + l : 3 * N + l + 1, :].astype(bf16)

    pl.when(core == 1)(lambda: put(own, got))
    pl.when(core == 0)(lambda: put(got, own))


def swap(x, axis_bit):
    return lax.ppermute(x, "tm", [(i, i ^ (1 << axis_bit)) for i in range(lax.axis_size("tm"))])


def shift(x, by):
    return lax.ppermute(x, "panel", [(i, (i + by) % N) for i in range(N)])


def combined(own_is_cov, outs, x_pair, x_pick, ring_refs, sources, gate, side, sides):
    up, down = call(
        functools.partial(ring_kernel, sources),
        [struct(UP, W), struct(DOWN, W)],
        streaming(DOWN // W),
        *ring_refs,
        vmem=0,
        vmem_out=False,
    )
    up, down, gate = lax.optimization_barrier((up, down, gate))
    p1 = shift(up, 1)
    m1 = shift(down, -1)
    p1, m1, (vec_i, vec_j, side_refs) = lax.optimization_barrier((p1, m1, side(gate)))
    p2, m2 = shift(p1, 1), shift(m1, -1)
    p3, m3 = shift(p2, 1), shift(m2, -1)
    p4 = shift(p3[HALF : 2 * HALF], 1)
    m4 = shift(m3[0:HALF], -1)
    (x_here,) = call(
        functools.partial(assemble_kernel, x_pick),
        [struct(D, D)],
        (),
        *x_pair,
        m1,
        m2,
        m3,
        p1,
        p2,
        p3,
    )
    x_far = swap(x_here, 0)
    last_own = jnp.concatenate([m4[512:768], p4[0:256]], axis=0)
    last_far = swap(last_own, 0)
    return call(
        functools.partial(combine_kernel, own_is_cov, sides, len(side_refs)),
        outs,
        (
            pltpu.VMEM((D, D), bf16),
            pltpu.VMEM((D, D), bf16),
            pltpu.VMEM((D, D), bf16),
            pltpu.VMEM((2 * W + 16, D), bf16),
            pltpu.VMEM((2 * W + 16, D), bf16),
            pltpu.VMEM((2 * W, D), bf16),
            pltpu.VMEM((2 * N, W), f32),
            pltpu.VMEM((D, W), bf16),
            pltpu.VMEM((D, W), bf16),
            pltpu.SemaphoreType.DMA((26,)),
        ),
        last_own,
        last_far,
        vec_i,
        vec_j,
        *side_refs,
        x_here,
        x_far,
        down,
        m1,
        m2,
        m3,
        p1,
        p2,
        p3,
        m4,
        p4,
        vmem=4,
    )


def local(transition, drift, spread, belief, precision, probe_hosts, probe_values):
    core, odd, _ = place()
    near = odd == 0
    move, cov, info = transition[0], spread[0], precision[0]

    def side0(drift):
        first, own_vec = call(
            start_kernel,
            [struct(D + 2 * N, W), struct(2 * N, W)],
            (),
            move,
            drift,
            belief,
            probe_hosts,
            probe_values,
        )
        got = swap(first, 0)
        got_vec = got[D:]
        vec_i = jnp.where(core == 0, own_vec, got_vec)
        vec_j = jnp.where(core == 0, got_vec, own_vec)
        return vec_i, vec_j, (move, got, cov, info)

    out1, out2 = combined(
        False,
        [struct(D, W), struct(D + 2 * N, W)],
        (cov, info),
        lambda core, odd: core,
        (cov, info, move),
        lambda core, odd: (core, 2),
        drift,
        side0,
        lambda core, odd: (core, 3 - core),
    )
    far_a = lax.ppermute(
        out2, "tm", [(i, i + 1 if i % 4 == 1 else i - 2) for i in range(1, lax.axis_size("tm"), 2)]
    )
    far_x = lax.ppermute(
        out1, "tm", [(i, i ^ 2) for i in range(lax.axis_size("tm")) if i % 4 in (1, 2)]
    )
    got2 = swap(out2, 0)
    own_vec = out2[D:] + got2[D:]

    def side1(own_vec):
        rest = jnp.where((core == 1) & near, out2[:D], out1)
        bundle = swap(jnp.concatenate([rest, own_vec], axis=0), 1)
        far_vec = bundle[D:]
        vec_i = jnp.where(near, own_vec, far_vec)
        vec_j = jnp.where(near, far_vec, own_vec)
        return vec_i, vec_j, (out1, out2, got2, far_a, bundle)

    sources = {(1, 0): (0, 3), (1, 1): (4, 1), (0, 0): (4, 2), (0, 1): (0, 3)}
    sides = {(1, 0): (1, 4), (1, 1): (4, 0), (0, 0): (2, 0), (0, 1): (3, 4)}
    (own,) = combined(
        True,
        [struct(2 * D + 2 * N, W)],
        (out1, far_x),
        lambda core, odd: 1 ^ core ^ odd,
        (out1, out2, got2, far_a, far_x),
        lambda core, odd: sources[core, odd],
        own_vec,
        side1,
        lambda core, odd: sides[core, odd],
    )
    got = swap(own, 0)
    panel = struct(D, W)
    row = struct(1, D)
    drift, belief, move, cov, info = call(
        finish_kernel,
        [row, row, panel, panel, panel],
        streaming(3 * N) + (pltpu.VMEM((4 * N, W), bf16), pltpu.SemaphoreType.DMA((2,))),
        own,
        got,
        vmem=0,
        vmem_out=[True, True, False, False, False],
    )
    return move[None], drift, cov[None], belief, info[None]


def solution(mesh):
    in_specs = (
        P("tm", None, "panel"),
        P("tm", None),
        P("tm", None, "panel"),
        P("tm", None),
        P("tm", None, "panel"),
        P("tm", None),
        P("tm", None),
    )
    out_specs = (
        P("tm", None, "panel"),
        P("tm", None),
        P("tm", None, "panel"),
        P("tm", None),
        P("tm", None, "panel"),
    )
    return jax.shard_map(local, mesh=mesh, in_specs=in_specs, out_specs=out_specs, check_vma=False)
```

```python
import functools

import jax
import jax.numpy as jnp
from jax import lax
from jax.experimental import pallas as pl
from jax.experimental.pallas import tpu as pltpu
from jax.sharding import PartitionSpec as P


NS = 2
W = 128
N = 8
D = W * N
RING = 1664
HALF = 768
INTERPRET = False

f32 = jnp.float32
bf16 = jnp.bfloat16


def dot(a, b):
    return jnp.dot(a, b, preferred_element_type=f32)


def call(kernel, out_shape, scratch, *args, vmem=None, vmem_out=True):
    vm = pl.BlockSpec(memory_space=pltpu.VMEM)
    hbm = pl.BlockSpec(memory_space=pl.ANY)
    staged = len(args) if vmem is None else vmem
    flags = vmem_out if isinstance(vmem_out, list) else [vmem_out] * len(out_shape)
    return pl.pallas_call(
        kernel,
        out_shape=list(out_shape),
        in_specs=[vm] * staged + [hbm] * (len(args) - staged),
        out_specs=[vm if flag else hbm for flag in flags],
        scratch_shapes=list(scratch),
        compiler_params=pltpu.CompilerParams(vmem_limit_bytes=56 * 2**20),
        interpret=INTERPRET,
    )(*args)


def place():
    t = lax.axis_index("tm").astype(jnp.int32)
    return t & 1, (t >> 1) & 1, lax.axis_index("panel").astype(jnp.int32)


def each_state(run):
    core, odd, _ = place()
    for i in (0, 1):
        for j in (0, 1):
            pl.when((core == i) & (odd == j))(lambda i=i, j=j: run(i, j))


def stream(pieces, buf, sems_in, sems_out):
    ins = [
        pltpu.make_async_copy(src.at[pl.ds(a, W)], buf.at[pl.ds(k * W, W)], sems_in.at[k])
        for k, (src, a, _, _) in enumerate(pieces)
    ]
    outs = [
        pltpu.make_async_copy(buf.at[pl.ds(k * W, W)], dst.at[pl.ds(b, W)], sems_out.at[k])
        for k, (_, _, dst, b) in enumerate(pieces)
    ]
    for c in ins:
        c.start()
    for c, o in zip(ins, outs):
        c.wait()
        o.start()
    for o in outs:
        o.wait()


def streaming(pieces):
    return (
        pltpu.VMEM((pieces * W, W), bf16),
        pltpu.SemaphoreType.DMA((pieces,)),
        pltpu.SemaphoreType.DMA((pieces,)),
    )


def struct(*shape):
    return jax.ShapeDtypeStruct(shape, bf16)


def at(index):
    return pl.multiple_of(index * W, W)


def blk(index):
    return pl.ds(at(index), W)


def start_kernel(move, drift, belief, hosts, values, msg, own_vec):
    msg[0:D, :] = move[...]
    eye = lax.broadcasted_iota(jnp.int32, (W, W), 0) == lax.broadcasted_iota(jnp.int32, (W, W), 1)

    def column(row):
        return jnp.sum(jnp.where(eye, row, 0.0), axis=1, keepdims=True)

    lane = lax.broadcasted_iota(jnp.int32, (W, W), 1).astype(f32)
    sums = [jnp.zeros((1, W), f32)] * N
    for c in range(hosts.shape[1] // W):
        part = slice(c * W, (c + 1) * W)
        spot = column(2.0 * hosts[:, part].astype(f32))
        value = column(values[:, part])
        for k in range(N):
            hit = jnp.where(spot == lane + k * W, value, 0.0)
            sums[k] = sums[k] + jnp.sum(hit, axis=0, keepdims=True)
    eta = belief[...].astype(f32) + jnp.concatenate(sums, axis=1)
    eta = eta.astype(bf16).astype(f32)
    b = drift[...].astype(f32)
    rows = [b[:, k * W : (k + 1) * W] for k in range(N)] + [
        eta[:, k * W : (k + 1) * W] for k in range(N)
    ]
    vec = jnp.concatenate(rows, axis=0).astype(bf16)
    msg[D : D + 2 * N, :] = vec
    own_vec[...] = vec


def ring_kernel(sources, *refs):
    *inputs, msg, buf, sems_in, sems_out = refs
    q = place()[2]

    def run(core, odd):
        x, a = (inputs[k] for k in sources(core, odd))
        spots = [(a, k * W, k * W if k < 4 else 512 + k * W) for k in range(N)]
        spots += [(x, at((q + d) % N), 512 + d * W) for d in range(4)]
        spots += [(x, at((q + 4) % N), 1536)]
        stream([(src, row, msg, to) for src, row, to in spots], buf, sems_in, sems_out)

    each_state(run)


def assemble_kernel(pick, xa, xb, m1, m2, m3, p1, p2, p3, x_out):
    core, odd, q = place()

    def put(l, d, block):
        r = (l + d) % N
        x_out[r * W : (r + 1) * W, l * W : (l + 1) * W] = block
        if d:
            x_out[l * W : (l + 1) * W, r * W : (r + 1) * W] = block.T

    def own(src):
        for d in range(N):
            put(0, d, src[blk((q + d) % N), :])

    pl.when(pick(core, odd) == 0)(lambda: own(xa))
    pl.when(pick(core, odd) == 1)(lambda: own(xb))
    for l, src in ((1, m1), (2, m2), (3, m3), (7, p1), (6, p2), (5, p3)):
        for d in range(5 if l < 4 else 4):
            if (l + d) % N == 0:
                continue
            row = 1536 if d == 4 else 512 + d * W
            put(l, d, src[row : row + W, :])
    x_out[4 * W :, 4 * W : 5 * W] = jnp.zeros((4 * W, W), bf16)
    x_out[4 * W : 5 * W, 5 * W :] = jnp.zeros((W, 3 * W), bf16)


def patch(dst, last):
    for d in range(4):
        block = last[d * W : (d + 1) * W, :]
        dst[(4 + d) * W : (5 + d) * W, 4 * W : 5 * W] = block
        if d:
            dst[4 * W : 5 * W, (4 + d) * W : (5 + d) * W] = block.T


def combine_kernel(own_is_cov, sides, count, last_own, last_far, vec_i, vec_j, *refs):
    side_refs = refs[:count]
    joined = len(refs) == count + 22
    if joined:
        out1 = refs[count + 11].at[pl.ds(0, D)]
        out2 = refs[count + 11].at[pl.ds(D, D + 2 * N)]
        refs = refs[: count + 11] + (out1, out2) + refs[count + 12 :]
    (x_here, x_far, msg, m1, m2, m3, p1, p2, p3, m4, p4, out1, out2,
     x_own, x_other, a_full, r, t, base, vecs, ai, add, sems) = refs[count:]
    core, _, q = place()
    terms = 2**NS - 1

    def whole(src, dst, first):
        return [
            pltpu.make_async_copy(
                src.at[pl.ds(k * 256, 256)], dst.at[pl.ds(k * 256, 256)], sems.at[first + k]
            )
            for k in range(4)
        ]

    own_copies = whole(x_here, x_own, 18)
    far_copies = whole(x_far, x_other, 22)
    copies = []
    for l, src in ((0, msg), (1, m1), (2, m2), (3, m3), (7, p1), (6, p2), (5, p3)):
        for half in range(2):
            copies.append((src, 1024 * half, 512 * half, l))
    copies += [(m4, 0, 0, 4), (p4, 256, 512, 4)]
    copies = [
        pltpu.make_async_copy(
            src.at[pl.ds(first, 512)], a_full.at[pl.ds(to, 512), pl.ds(l * W, W)], sems.at[2 + i]
        )
        for i, (src, first, to, l) in enumerate(copies)
    ]
    side_copies = [
        pltpu.make_async_copy(side_refs[0].at[pl.ds(0, D)], dst, sems.at[k])
        for k, dst in enumerate((ai, add))
    ]

    def start_sides(i, j):
        for k, dst in zip(sides(i, j), (ai, add)):
            sem = sems.at[0] if dst is ai else sems.at[1]
            pltpu.make_async_copy(side_refs[k].at[pl.ds(0, D)], dst, sem).start()

    each_state(start_sides)

    def start(group):
        for c in group:
            c.start()

    def wait(group):
        for c in group:
            c.wait()

    top_half = q < N // 2
    halves = copies[0::2], copies[1::2]

    def by_half(act, first):
        pl.when(top_half)(lambda: act(halves[0 if first else 1]))
        pl.when(jnp.logical_not(top_half))(lambda: act(halves[1 if first else 0]))

    @pl.when(core == 1)
    def _():
        by_half(start, True)
        start(own_copies if own_is_cov else far_copies)
        start(far_copies if own_is_cov else own_copies)
        by_half(start, False)

    @pl.when(core == 0)
    def _():
        start(own_copies if own_is_cov else far_copies)
        start(far_copies if own_is_cov else own_copies)
        start(copies)

    vi = vec_i[...].astype(f32)
    vj = vec_j[...].astype(f32)

    def ready_own():
        wait(own_copies)
        patch(x_own, last_own)

    def ready_far():
        wait(far_copies)
        patch(x_other, last_far)

    first_ready, then_ready = (ready_own, ready_far) if own_is_cov else (ready_far, ready_own)
    first_x, then_x = (x_own, x_other) if own_is_cov else (x_other, x_own)

    def rotated_move(dst, row):
        for l in range(N):
            dst[row : row + W, l * W : (l + 1) * W] = ai[blk((q + l) % N), :].T

    def rotated_vector(rows, first):
        vecs[...] = rows
        return jnp.concatenate([vecs[pl.ds(first + (q + l) % N, 1), :] for l in range(N)], axis=1)

    def as_rows(vector):
        return jnp.broadcast_to(vector, (16, D)).astype(bf16)

    @pl.when(core == 1)
    def _():
        cov, info = first_x, then_x
        eta = rotated_vector(vj, N)
        w = rotated_vector(vi, 0)
        side_copies[0].wait()
        rotated_move(base, W)
        r[W : W + 16, :] = as_rows(eta)
        by_half(wait, True)
        r[0:W, :] = a_full[blk(q), :]
        first_ready()
        out = dot(r[0 : W + 16, :], cov[...])
        base[0:W, :] = out[0:W].astype(bf16)
        w = w + out[W : W + 1]
        r[0 : 2 * W, :] = base[...]
        r[2 * W : 2 * W + 16, :] = as_rows(w)
        then_ready()
        for _ in range(terms):
            t[...] = dot(r[...], info[...]).astype(bf16)
            out = dot(t[...], cov[...])
            r[0 : 2 * W, :] = (base[...].astype(f32) - out[0 : 2 * W]).astype(bf16)
            r[2 * W : 2 * W + 16, :] = as_rows(w - out[2 * W : 2 * W + 1])
        by_half(wait, False)
        res = lax.dot_general(
            r[...], a_full[...], (((1,), (1,)), ((), ())), preferred_element_type=f32
        )
        side_copies[1].wait()
        for l in range(N):
            rows = slice(l * W, (l + 1) * W)
            out1[rows, :] = (res[0:W, rows].T + add[rows, :].astype(f32)).astype(bf16)
            out2[rows, :] = res[W : 2 * W, rows].astype(bf16).T
        rows = [res[2 * W : 2 * W + 1, l * W : (l + 1) * W] + vj[l : l + 1, :] for l in range(N)]
        rows = rows + [jnp.zeros((1, W), f32)] * N
        out2[D : D + 2 * N, :] = jnp.concatenate(rows, axis=0).astype(bf16)

    @pl.when(core == 0)
    def _():
        info, cov = first_x, then_x
        top = slice(0, W)
        low = slice(W, W + 16)
        both = slice(0, W + 16)
        eta = rotated_vector(vj, N)
        side_copies[0].wait()
        rotated_move(base, 0)
        r[top, :] = base[top, :]
        r[low, :] = as_rows(rotated_vector(vi, 0))
        first_ready()
        out = dot(r[both, :], info[...])
        start_vec = eta - out[W : W + 1]
        t[top, :] = out[top].astype(bf16)
        t[low, :] = as_rows(start_vec)
        then_ready()
        for _ in range(terms):
            out = dot(t[both, :], cov[...])
            r[top, :] = (base[top, :].astype(f32) - out[top]).astype(bf16)
            r[low, :] = out[low].astype(bf16)
            out = dot(r[both, :], info[...])
            t[top, :] = out[top].astype(bf16)
            t[low, :] = as_rows(start_vec - out[W : W + 1])
        wait(copies)
        side_copies[1].wait()
        for l in range(N):
            x_other[blk((q + l) % N), 0 : W + 16] = t[both, l * W : (l + 1) * W].T
        for l in range(N):
            r[both, l * W : (l + 1) * W] = x_other[l * W : (l + 1) * W, 0 : W + 16].T
        res = dot(r[both, :], a_full[...])
        for l in range(N):
            rows = blk((q + l) % N)
            out1[rows, :] = (res[top, l * W : (l + 1) * W].T + add[rows, :].astype(f32)).astype(bf16)
        vecs[...] = vi
        for l in range(N):
            spot = pl.ds(N + (q + l) % N, 1)
            vecs[spot, :] = vecs[spot, :] + res[W : W + 1, l * W : (l + 1) * W]
        rows = lax.broadcasted_iota(jnp.int32, (2 * N, W), 0)
        out2[0:D, :] = jnp.zeros((D, W), bf16)
        out2[D : D + 2 * N, :] = jnp.where(rows < N, 0.0, vecs[...]).astype(bf16)


def finish_kernel(own, got, drift, belief, move, spread, weight):
    core = place()[0]

    def put(early, late):
        spread[...] = early[0:D, :]
        move[...] = early[D : 2 * D, :]
        weight[...] = late[0:D, :]
        b = early[2 * D : 2 * D + 2 * N, :].astype(f32)
        e = late[2 * D : 2 * D + 2 * N, :].astype(f32)
        for l in range(N):
            drift[:, l * W : (l + 1) * W] = b[l : l + 1, :].astype(bf16)
            belief[:, l * W : (l + 1) * W] = e[N + l : N + l + 1, :].astype(bf16)

    pl.when(core == 1)(lambda: put(own, got))
    pl.when(core == 0)(lambda: put(got, own))


def swap(x, axis_bit):
    return lax.ppermute(x, "tm", [(i, i ^ (1 << axis_bit)) for i in range(lax.axis_size("tm"))])


def shift(x, by):
    return lax.ppermute(x, "panel", [(i, (i + by) % N) for i in range(N)])


def combined(own_is_cov, outs, x_pair, x_pick, ring_refs, sources, gate, side, sides):
    (msg,) = call(
        functools.partial(ring_kernel, sources),
        [struct(RING, W)],
        streaming(RING // W),
        *ring_refs,
        vmem=0,
        vmem_out=False,
    )
    msg, gate = lax.optimization_barrier((msg, gate))
    p1 = shift(msg, 1)
    m1 = shift(msg, -1)
    p2, m2 = shift(p1, 1), shift(m1, -1)
    p2, (vec_i, vec_j, side_refs) = lax.optimization_barrier((p2, side(gate)))
    p3, m3 = shift(p2, 1), shift(m2, -1)
    p4 = shift(p3[HALF : 2 * HALF], 1)
    m4 = shift(m3[0:HALF], -1)
    (x_here,) = call(
        functools.partial(assemble_kernel, x_pick),
        [struct(D, D)],
        (),
        *x_pair,
        m1,
        m2,
        m3,
        p1,
        p2,
        p3,
    )
    x_far = swap(x_here, 0)
    last_own = jnp.concatenate([m4[512:768], p4[0:256]], axis=0)
    last_far = swap(last_own, 0)
    return call(
        functools.partial(combine_kernel, own_is_cov, sides, len(side_refs)),
        outs,
        (
            pltpu.VMEM((D, D), bf16),
            pltpu.VMEM((D, D), bf16),
            pltpu.VMEM((D, D), bf16),
            pltpu.VMEM((2 * W + 16, D), bf16),
            pltpu.VMEM((2 * W + 16, D), bf16),
            pltpu.VMEM((2 * W, D), bf16),
            pltpu.VMEM((2 * N, W), f32),
            pltpu.VMEM((D, W), bf16),
            pltpu.VMEM((D, W), bf16),
            pltpu.SemaphoreType.DMA((26,)),
        ),
        last_own,
        last_far,
        vec_i,
        vec_j,
        *side_refs,
        x_here,
        x_far,
        msg,
        m1,
        m2,
        m3,
        p1,
        p2,
        p3,
        m4,
        p4,
        vmem=4,
    )


def local(transition, drift, spread, belief, precision, probe_hosts, probe_values):
    core, odd, _ = place()
    near = odd == 0
    move, cov, info = transition[0], spread[0], precision[0]

    def side0(drift):
        first, own_vec = call(
            start_kernel,
            [struct(D + 2 * N, W), struct(2 * N, W)],
            (),
            move,
            drift,
            belief,
            probe_hosts,
            probe_values,
        )
        got = swap(first, 0)
        got_vec = got[D:]
        vec_i = jnp.where(core == 0, own_vec, got_vec)
        vec_j = jnp.where(core == 0, got_vec, own_vec)
        return vec_i, vec_j, (move, got, cov, info)

    out1, out2 = combined(
        False,
        [struct(D, W), struct(D + 2 * N, W)],
        (cov, info),
        lambda core, odd: core,
        (cov, info, move),
        lambda core, odd: (core, 2),
        drift,
        side0,
        lambda core, odd: (core, 3 - core),
    )
    far_a = lax.ppermute(
        out2, "tm", [(i, i + 1 if i % 4 == 1 else i - 2) for i in range(1, lax.axis_size("tm"), 2)]
    )
    far_x = lax.ppermute(
        out1, "tm", [(i, i ^ 2) for i in range(lax.axis_size("tm")) if i % 4 in (1, 2)]
    )
    got2 = swap(out2, 0)
    own_vec = out2[D:] + got2[D:]

    def side1(own_vec):
        rest = jnp.where((core == 1) & near, out2[:D], out1)
        bundle = swap(jnp.concatenate([rest, own_vec], axis=0), 1)
        far_vec = bundle[D:]
        vec_i = jnp.where(near, own_vec, far_vec)
        vec_j = jnp.where(near, far_vec, own_vec)
        return vec_i, vec_j, (out1, out2, got2, far_a, bundle)

    sources = {(1, 0): (0, 3), (1, 1): (4, 1), (0, 0): (4, 2), (0, 1): (0, 3)}
    sides = {(1, 0): (1, 4), (1, 1): (4, 0), (0, 0): (2, 0), (0, 1): (3, 4)}
    (own,) = combined(
        True,
        [struct(2 * D + 2 * N, W)],
        (out1, far_x),
        lambda core, odd: 1 ^ core ^ odd,
        (out1, out2, got2, far_a, far_x),
        lambda core, odd: sources[core, odd],
        own_vec,
        side1,
        lambda core, odd: sides[core, odd],
    )
    got = swap(own, 0)
    panel = struct(D, W)
    row = struct(1, D)
    drift, belief, move, cov, info = call(
        finish_kernel,
        [row, row, panel, panel, panel],
        (),
        own,
        got,
    )
    return move[None], drift, cov[None], belief, info[None]


def solution(mesh):
    in_specs = (
        P("tm", None, "panel"),
        P("tm", None),
        P("tm", None, "panel"),
        P("tm", None),
        P("tm", None, "panel"),
        P("tm", None),
        P("tm", None),
    )
    out_specs = (
        P("tm", None, "panel"),
        P("tm", None),
        P("tm", None, "panel"),
        P("tm", None),
        P("tm", None, "panel"),
    )
    return jax.shard_map(local, mesh=mesh, in_specs=in_specs, out_specs=out_specs, check_vma=False)
```
